256 devices in a mesh: row: 8 (over z), col: 32 (over y, x, core).
Axes of the slice: x: 4, y: 4, z: 8, core: 2. Of those that a mesh axis runs over, the one named last changes fastest.
Arguments:
- tiles: bfloat16 [8, 32, 16, 576, 576], P('row', 'col'), may hold values from -0.0625 to 0.0625
- diag_tiles: bfloat16 [256, 576, 576], P(('row', 'col')), as said below
- probes: float32 [256, 64, 576], P(('row', 'col'))
- rows_list: int32 [8, 32, 16], P('row', 'col'), may hold values from 0 to 31, as said below
- cols_list: int32 [8, 32, 16], P('row', 'col'), may hold values from 0 to 7, as said below
- counts: int32 [8, 32], P('row', 'col'), may hold values from 0 to 16, as said below
Outputs:
- solution: float32 [256, 64, 576], P(('row', 'col'))
- residual: float32 [256, 64, 576], P(('row', 'col'))
The draws below stay inside these ranges and needn't reach their ends.
Inputs may be any that keep to these rules, and one draw needn't show every extreme that they name: `rows_list`: slots past a device's count hold 0; a held slot lies strictly below the diagonal. `cols_list`: slots past a device's count hold 0. `counts`: the busiest device holds 16 tiles. `diag_tiles`: each diagonal tile is symmetric positive definite: its diagonal entries are at least 4.4 and its off-diagonal part has spectral radius below about 1.
All inputs are finite; a program needn't handle non-finite values.
Results may differ from the reference program's by a relative error of at most 0.039.
Values may be sent and summed in bfloat16 or wider, within the bound.
A program may use at most 128 MiB of HBM per device.

```python
import math
import jax
import jax.numpy as jnp
from jax import lax

B = 576
P_SIZE = 64
KMAX = 16
ITERS = 2
ROW_BLOCKS = 8
COL_BLOCKS = 32
NT = 256


def tile_lists(key):
    keys = jax.random.split(jax.random.fold_in(key, 7), 3)
    shape = (ROW_BLOCKS, COL_BLOCKS, KMAX)
    rows = jnp.arange(ROW_BLOCKS)[:, None, None]
    cols = jnp.arange(COL_BLOCKS)[None, :, None]
    slots = jnp.arange(KMAX)[None, None, :]
    first = jax.random.randint(keys[0], shape, 0, 1 << 20)
    second = jax.random.randint(keys[1], shape, 0, 1 << 20)
    third = jax.random.randint(keys[2], (ROW_BLOCKS, COL_BLOCKS), 0, 1 << 20)
    lastcol = cols == COL_BLOCKS - 1
    source = first % (rows + 1)
    source = jnp.where((source == rows) & lastcol, rows - 1, source)
    forced = (rows == ROW_BLOCKS - 1) & (cols == 0) & (slots == 0)
    source = jnp.where(forced, ROW_BLOCKS - 1, source)
    room = jnp.maximum(COL_BLOCKS - 1 - cols, 1)
    local = jnp.where(source == rows, cols + 1 + second % room, second % COL_BLOCKS)
    rr = jnp.arange(ROW_BLOCKS)[:, None]
    cc = jnp.arange(COL_BLOCKS)[None, :]
    count = jnp.maximum(1, KMAX * (rr + 1) // ROW_BLOCKS - third % 2)
    count = jnp.where((rr == ROW_BLOCKS - 1) & (cc == 0), KMAX, count)
    count = jnp.where((rr == 0) & (cc == COL_BLOCKS - 1), 0, count)
    held = slots < count[:, :, None]
    local = jnp.where(held, local, 0)
    source = jnp.where(held, source, 0)
    return (local.astype(jnp.int32), source.astype(jnp.int32), count.astype(jnp.int32))


def draw_rows_list(key, part):
    return tile_lists(key)[0]


def draw_cols_list(key, part):
    return tile_lists(key)[1]


def draw_counts(key, part):
    return tile_lists(key)[2]


def draw_diag_tiles(key, part):
    keys = jax.random.split(jax.random.fold_in(key, 11), 2)
    noise = jax.random.normal(keys[0], (NT, B, B), jnp.float32) * (0.5 / math.sqrt(B))
    lift = jax.random.uniform(keys[1], (NT, B), jnp.float32, 5.0, 7.0)
    sym = 0.5 * (noise + jnp.swapaxes(noise, 1, 2))
    full = sym + jnp.eye(B, dtype=jnp.float32)[None, :, :] * lift[:, None, :]
    return full.astype(jnp.bfloat16)


def draw_probes(key, part):
    keys = jax.random.split(jax.random.fold_in(key, 13), 1)
    ramp = 1.0 + 2.0 * jnp.arange(NT, dtype=jnp.float32) / (NT - 1)
    values = jax.random.normal(keys[0], (NT, P_SIZE, B), jnp.float32)
    return values * ramp[:, None, None]


def shard_levels(key, dims, cuts, smallest, high):
    level, own = 1.0, jax.random.fold_in(key, 6)
    for axis_at, blocks in cuts:
        draws = jnp.exp(jax.random.uniform(jax.random.fold_in(own, axis_at), (blocks,), jnp.float32, smallest / len(cuts), high / len(cuts)))
        level = level * jnp.repeat(draws, dims[axis_at] // blocks).reshape([-1 if axis == axis_at else 1 for axis in range(len(dims))])
    return level


def centred(key, extent, width, limit, shards=(), kind=jnp.bfloat16):
    result = jax.random.normal(key, extent, jnp.float32) * width
    if len(shards) > 0:
        result = shard_levels(key, extent, shards, -0.22, 0.18) * result
    return jnp.clip(result, min=-limit, max=limit).astype(kind)


def setup_inputs(seed: int = 0) -> dict:
    key_of = jax.random.split(jax.random.key(seed), 7)
    tiles = centred(key_of[0], (ROW_BLOCKS, COL_BLOCKS, KMAX, B, B), (16 * B) ** -0.5, 0.0625, ((0, 8), (1, 32)))
    diag_tiles = draw_diag_tiles(jax.random.fold_in(key_of[6], 71), 0)
    probes = draw_probes(jax.random.fold_in(key_of[6], 71), 0)
    rows_list = draw_rows_list(jax.random.fold_in(key_of[6], 71), 0)
    cols_list = draw_cols_list(jax.random.fold_in(key_of[6], 71), 0)
    counts = draw_counts(jax.random.fold_in(key_of[6], 71), 0)
    return {"tiles": tiles, "diag_tiles": diag_tiles, "probes": probes, "rows_list": rows_list, "cols_list": cols_list, "counts": counts}


def gram(left, right):
    return jnp.einsum('tpb,tqb->pq', left, right, precision=lax.Precision.HIGHEST)

def combine(coef, block):
    return jnp.einsum('pq,tpb->tqb', coef, block, precision=lax.Precision.HIGHEST)

def solve_with(matrix, rhs):
    factor = jnp.linalg.cholesky(matrix)
    middle = lax.linalg.triangular_solve(factor, rhs, left_side=True, lower=True, transpose_a=False)
    return lax.linalg.triangular_solve(factor, middle, left_side=True, lower=True, transpose_a=True)

def operator(tiles, diag_tiles, rows_list, cols_list, counts, direction):
    rounded = direction.astype(jnp.bfloat16)
    slots = jnp.arange(KMAX)

    def visit(acc, dev):
        r = dev // COL_BLOCKS
        c = dev % COL_BLOCKS
        blocks = tiles[r, c].astype(jnp.float32)
        valid = (slots < counts[r, c]).astype(jnp.float32)[:, None, None]
        grow = (r * COL_BLOCKS + rows_list[r, c]).astype(jnp.int32)
        gcol = (cols_list[r, c] * COL_BLOCKS + c).astype(jnp.int32)
        near = rounded[grow].astype(jnp.float32)
        far = rounded[gcol].astype(jnp.float32)
        fwd = jnp.einsum('kpb,kcb->kpc', far, blocks) * valid
        bwd = jnp.einsum('kpb,kbc->kpc', near, blocks) * valid
        acc = acc.at[grow].add(fwd)
        acc = acc.at[gcol].add(bwd)
        own = lax.dot_general(rounded[dev].astype(jnp.float32), diag_tiles[dev].astype(jnp.float32), (((1,), (1,)), ((), ())), preferred_element_type=jnp.float32)
        acc = acc.at[dev].add(own)
        return (acc, None)
    start = jnp.zeros(direction.shape, jnp.float32)
    image, unused = lax.scan(visit, start, jnp.arange(NT).astype(jnp.int32))
    return image

def reference(tiles, diag_tiles, probes, rows_list, cols_list, counts):
    solution = jnp.zeros(probes.shape, jnp.float32)
    residual = probes
    direction = probes
    norm_now = gram(residual, residual)
    for step in range(ITERS):
        image = operator(tiles, diag_tiles, rows_list, cols_list, counts, direction)
        curv = gram(direction, image)
        alpha = solve_with(curv, norm_now)
        solution = solution + combine(alpha, direction)
        residual = residual - combine(alpha, image)
        if step + 1 < ITERS:
            norm_next = gram(residual, residual)
            beta = solve_with(norm_now, norm_next)
            direction = residual + combine(beta, direction)
            norm_now = norm_next
    return (solution, residual)
```

```python
import jax
import jax.numpy as jnp
from jax import lax
from jax.experimental import pallas as pl
from jax.experimental.pallas import tpu as pltpu
from jax.sharding import PartitionSpec as P

MESH = pl.DeviceIdType.MESH
B, Q, SLOTS, ROWS, PLANE = 576, 64, 16, 8, 32
PK, HALF = 288, 144
STEPS = (1, 3, 2)
N_COPIES = 220
NT = 256


def pack(v):
    tail = jnp.concatenate([v[0:32, 512:576], v[32:64, 512:576]], axis=1)
    return jnp.concatenate(
        [v[:, 0:128], v[:, 128:256], v[:, 256:384], v[:, 384:512], tail], axis=0
    )


def unpack(w):
    tail = jnp.concatenate([w[256:288, 0:64], w[256:288, 64:128]], axis=0)
    return jnp.concatenate(
        [w[0:64], w[64:128], w[128:192], w[192:256], tail], axis=1
    )


def dot(a, b, ca, cb):
    return lax.dot_general(
        a, b, (((ca,), (cb,)), ((), ())), preferred_element_type=jnp.float32
    )


def dot_hi(a, b, ca, cb):
    return lax.dot_general(
        a, b, (((ca,), (cb,)), ((), ())),
        precision=lax.Precision.HIGHEST, preferred_element_type=jnp.float32,
    )


def gram(a, b):
    return dot_hi(a, b, 1, 1)


def combine(coef, block):
    return dot_hi(coef, block, 0, 0)


def solve(matrix, rhs):
    i = lax.broadcasted_iota(jnp.int32, (Q, Q), 0)
    j = lax.broadcasted_iota(jnp.int32, (Q, Q), 1)
    sym = jnp.where(i >= j, matrix, matrix.T)
    work = jnp.concatenate([sym, rhs], axis=1)
    lane = lax.broadcasted_iota(jnp.int32, (Q, 2 * Q), 0)
    for k in range(Q):
        row = work[k : k + 1, :] * (1.0 / work[k : k + 1, k : k + 1])
        work = jnp.where(lane == k, row, work - work[:, k : k + 1] * row)
    return work[:, Q:]


def kernel(
    rows_ref, cols_ref, counts_ref, tiles_ref, diag_ref, probes_ref,
    sol_ref, res_ref,
    blocks, diag, rp_a, rp_b, cp_a, cp_b, ps, xb, qb, r1, sb, r2, pz, zq, zr1, zh, zr2,
    seg_r, seg_c, prev_r, prev_c, last_r, last_c,
    ar0, ar0r, ar1, ar1r, ar2, ar2r,
    send_sem, recv_sem, tile_sem, diag_sem,
):
    z = lax.axis_index("row")
    c = lax.axis_index("col")
    y, x, k = c // 8, (c // 2) % 4, c % 2

    def at(dz=0, dy=0, dx=0, flip=False):
        kk = 1 - k if flip else k
        return (
            lax.rem(z + dz + 8, 8),
            (lax.rem(y + dy + 4, 4) * 4 + lax.rem(x + dx + 4, 4)) * 2 + kk,
        )

    def wrap(v, n):
        return lax.rem(v + 2 * n, n)

    plane_of = {0: lambda d: at(dx=d), 1: lambda d: at(dy=d)}
    used = []
    rps, cps = (rp_a, rp_b), (cp_a, cp_b)

    def send(src, dst, device):
        i = len(used)
        copy = pltpu.make_async_remote_copy(
            src_ref=src, dst_ref=dst, send_sem=send_sem.at[i], recv_sem=recv_sem.at[i],
            device_id=device, device_id_type=MESH,
        )
        used.append(copy)
        copy.start()
        return copy

    tile_copies = [
        pltpu.make_async_copy(tiles_ref.at[0, 0, s], blocks.at[s], tile_sem.at[s])
        for s in range(SLOTS)
    ]
    diag_copy = pltpu.make_async_copy(diag_ref.at[0], diag, diag_sem.at[0])
    diag_copy.start()
    for copy in tile_copies:
        copy.start()

    peers = [at(dx=d) for d in STEPS] + [at(dy=d) for d in STEPS]
    peers += [at(dz=d) for d in range(1, 8)] + [at(flip=True)]
    barrier = pltpu.get_barrier_semaphore()
    for peer in peers:
        pl.semaphore_signal(barrier, inc=1, device_id=peer, device_id_type=MESH)
    pl.semaphore_wait(barrier, len(peers))

    def half(h):
        return pl.ds(h * HALF, HALF)

    def gather_begin(p, value):
        rps[p][k, y, x] = value
        cps[p][z] = value
        first, second, far = [], [], []
        for h in range(2):
            own = rps[p].at[k, y, x, half(h)]
            first.append([send(own, own, plane_of[h](d)) for d in STEPS])
        own = cps[p].at[z]
        for d in (2, -2, 1, -1):
            far.append(send(own, own, at(dz=d)))
        for h in range(2):
            own = rps[p].at[k, y, x, half(h)]
            second.append([[send(own, own, plane_of[1 - h](e)) for e in STEPS]])
        return first, second, far

    def gather_forward(p, state):
        first, second, far = state
        for i, d in enumerate(STEPS):
            for h in range(2):
                first[h][i].wait_recv()
                ty, tx = (y, wrap(x - d, 4)) if h == 0 else (wrap(y - d, 4), x)
                got = rps[p].at[k, ty, tx, half(h)]
                second[h].append([send(got, got, plane_of[1 - h](e)) for e in STEPS])
        for i, d in enumerate((2, -2)):
            far[i].wait_recv()
            got = cps[p].at[wrap(z - d, 8)]
            far.append(send(got, got, at(dz=d // 2)))
            got = cps[p].at[wrap(z - d, 8), half(i)]
            far.append(send(got, got, at(dz=d)))
        third = []
        for h in range(2):
            group = rps[p].at[k, y, :, half(h)] if h == 0 else rps[p].at[k, :, x, half(h)]
            third.append(send(group, group, at(flip=True)))
        return first, second, far, third

    def gather_across(p, state):
        first, second, far, third = state
        for j, e in enumerate(STEPS):
            for h in range(2):
                for part in second[h]:
                    part[j].wait_recv()
                group = (
                    rps[p].at[k, wrap(y - e, 4), :, half(h)]
                    if h == 0
                    else rps[p].at[k, :, wrap(x - e, 4), half(h)]
                )
                third.append(send(group, group, at(flip=True)))

    def gather_end_z(state):
        far = state[2]
        for copy in far[2:]:
            copy.wait_recv()

    def gather_end_plane(state):
        for copy in state[3]:
            copy.wait_recv()

    def forward_products(p):
        @pl.loop(0, SLOTS)
        def _(s):
            far = unpack(cps[p][cols_ref[0, 0, s]])
            seg_r[s] = pack(dot(far, blocks[s], 1, 1)) + seg_r[prev_r[s]]

    def mirror_products(p):
        @pl.loop(0, SLOTS)
        def _(s):
            t = rows_ref[0, 0, s]
            near = unpack(rps[p][lax.rem(t, 2), t // 8, lax.rem(t // 2, 4)])
            seg_c[s] = pack(dot(near, blocks[s], 1, 0)) + seg_c[prev_c[s]]

    def plane_begin(p):
        def fill(kk):
            @pl.loop(0, 16)
            def _(t):
                ps[p, kk, t // 4, lax.rem(t, 4)] = seg_r[last_r[2 * t + kk]].astype(jnp.bfloat16)

        fill(1 - k)
        out = []
        for e in (2, 1, 3, 0):
            for h in range(2):
                if h == 0:
                    t = wrap(y + e, 4)
                    src, dst = ps.at[p, 1 - k, t, :, half(h)], xb.at[p, t, :, half(h)]
                else:
                    t = wrap(x + e, 4)
                    src, dst = ps.at[p, 1 - k, :, t, half(h)], xb.at[p, :, t, half(h)]
                out.append(send(src, dst, at(flip=True)))
        fill(k)
        return out

    def plane_stage(p, across):
        out = [[], []]
        n = 0
        for e in (2, 1, 3, 0):
            for h in range(2):
                across[n].wait_recv()
                n += 1
                if h == 0:
                    t = wrap(y + e, 4)
                    total = ps[p, k, t, :, half(h)].astype(jnp.float32) + xb[p, t, :, half(h)].astype(jnp.float32)
                else:
                    t = wrap(x + e, 4)
                    total = ps[p, k, :, t, half(h)].astype(jnp.float32) + xb[p, :, t, half(h)].astype(jnp.float32)
                qb[p, h, e] = total.astype(jnp.bfloat16)
                if e != 0:
                    out[h].append(send(qb.at[p, h, e], r1.at[p, h, e - 1], plane_of[1 - h](e)))
        return out

    def plane_stage2(p, mid):
        out = [[], []]
        for h in range(2):
            for copy in mid[h]:
                copy.wait_recv()
            total = qb[p, h, 0].astype(jnp.float32)
            for e in range(3):
                total = total + r1[p, h, e].astype(jnp.float32)
            sb[p, h] = total.astype(jnp.bfloat16)
            at_axis = x if h == 0 else y
            for d in (1, 2, 3):
                out[h].append(send(sb.at[p, h, wrap(at_axis + d, 4)], r2.at[p, h, d - 1], plane_of[h](d)))
        return out

    def plane_end(p, last):
        halves = []
        for h in range(2):
            total = sb[p, h, x if h == 0 else y].astype(jnp.float32)
            for d in range(3):
                last[h][d].wait_recv()
                total = total + r2[p, h, d].astype(jnp.float32)
            halves.append(total)
        return jnp.concatenate(halves, axis=0)

    def z_begin(p):
        @pl.loop(0, ROWS)
        def _(t):
            pz[p, t] = seg_c[last_c[t]].astype(jnp.bfloat16)

        out = [
            send(pz.at[p, wrap(z + 3, 8)], zr1.at[p, 0], at(dz=1)),
            send(pz.at[p, wrap(z - 3, 8)], zr1.at[p, 1], at(dz=-1)),
            send(pz.at[p, wrap(z + 4, 8), half(0)], zh.at[p, 0], at(dz=2)),
            send(pz.at[p, wrap(z + 4, 8), half(1)], zh.at[p, 1], at(dz=-2)),
            send(pz.at[p, wrap(z + 1, 8)], zr2.at[p, 0], at(dz=1)),
            send(pz.at[p, wrap(z - 1, 8)], zr2.at[p, 1], at(dz=-1)),
        ]
        return out

    def z_stage(p, out):
        for i, d in enumerate((2, -2)):
            out[i].wait_recv()
            out[2 + i].wait_recv()
            total = pz[p, wrap(z + d, 8)].astype(jnp.float32) + zr1[p, i].astype(jnp.float32)
            extra = zh[p, i].astype(jnp.float32)
            lo, hi = total[0:HALF], total[HALF:PK]
            if i == 0:
                lo = lo + extra
            else:
                hi = hi + extra
            zq[p, i, 0:HALF] = lo.astype(jnp.bfloat16)
            zq[p, i, HALF:PK] = hi.astype(jnp.bfloat16)
            out.append(send(zq.at[p, i], zr2.at[p, 2 + i], at(dz=d)))

    def z_end(p, out):
        total = pz[p, z].astype(jnp.float32)
        for i in range(4):
            out[4 + i].wait_recv()
            total = total + zr2[p, i].astype(jnp.float32)
        return total

    groups = (
        [at(flip=True)],
        [at(dx=d) for d in STEPS],
        [at(dy=d) for d in STEPS],
        [at(dz=d) for d in range(1, 8)],
    )
    bases = (0, 1, 4, 7)

    def reduce_start(buf, rbuf, stage):
        return [
            send(buf.at[stage], rbuf.at[bases[stage] + i], peer)
            for i, peer in enumerate(groups[stage])
        ]

    def reduce_finish(buf, rbuf, stage, copies):
        total = buf[stage]
        for i, copy in enumerate(copies):
            copy.wait_recv()
            total = total + rbuf[bases[stage] + i]
        if stage < 3:
            buf[stage + 1] = total
        return total

    def own_product(v):
        hi = v.astype(jnp.bfloat16)
        lo = (v - hi.astype(jnp.float32)).astype(jnp.bfloat16)
        d = diag[...]
        return dot(hi, d, 1, 1) + dot(lo, d, 1, 1)

    probes = probes_ref[0]
    state = gather_begin(0, pack(probes).astype(jnp.bfloat16))

    count = counts_ref[0, 0]
    for s in range(SLOTS):
        pr = jnp.int32(SLOTS)
        pc = jnp.int32(SLOTS)
        for u in range(s):
            pr = jnp.where(rows_ref[0, 0, u] == rows_ref[0, 0, s], u, pr)
            pc = jnp.where(cols_ref[0, 0, u] == cols_ref[0, 0, s], u, pc)
        prev_r[s] = pr
        prev_c[s] = pc

    @pl.loop(0, PLANE)
    def _(t):
        at_slot = jnp.int32(SLOTS)
        for s in range(SLOTS):
            at_slot = jnp.where((rows_ref[0, 0, s] == t) & (s < count), s, at_slot)
        last_r[t] = at_slot

    @pl.loop(0, ROWS)
    def _(t):
        at_slot = jnp.int32(SLOTS)
        for s in range(SLOTS):
            at_slot = jnp.where((cols_ref[0, 0, s] == t) & (s < count), s, at_slot)
        last_c[t] = at_slot

    seg_r[SLOTS] = jnp.zeros((PK, 128), jnp.float32)
    seg_c[SLOTS] = jnp.zeros((PK, 128), jnp.float32)

    diag_copy.wait()
    own = own_product(probes)
    trace = jnp.float32(0.0)
    for j in range(5):
        n = 128 if j < 4 else 64
        d = diag[pl.ds(128 * j, n), pl.ds(128 * j, n)].astype(jnp.float32)
        eye = lax.broadcasted_iota(jnp.int32, (n, n), 0) == lax.broadcasted_iota(jnp.int32, (n, n), 1)
        trace = trace + jnp.sum(jnp.where(eye, d, 0.0), keepdims=True)
    g00 = gram(probes, probes)
    ar0[0, 0:64] = jnp.concatenate([g00, jnp.broadcast_to(trace, (Q, Q))], axis=1)
    red = reduce_start(ar0, ar0r, 0)
    state = gather_forward(0, state)
    reduce_finish(ar0, ar0r, 0, red)
    red = reduce_start(ar0, ar0r, 1)
    gather_across(0, state)
    gather_end_z(state)
    reduce_finish(ar0, ar0r, 1, red)
    red = reduce_start(ar0, ar0r, 2)
    for copy in tile_copies:
        copy.wait()
    forward_products(0)
    across = plane_begin(0)
    gather_end_plane(state)
    mirror_products(0)
    zs = z_begin(0)
    reduce_finish(ar0, ar0r, 2, red)
    red = reduce_start(ar0, ar0r, 3)
    mid = plane_stage(0, across)
    z_stage(0, zs)
    last = plane_stage2(0, mid)
    total = reduce_finish(ar0, ar0r, 3, red)
    rr0 = total[:, 0:Q]
    shift = total[0:1, Q : Q + 1] * (1.0 / (NT * B))
    image = z_end(0, zs)
    image = image + plane_end(0, last)
    image = own + unpack(image)
    basis = image - shift * probes

    state = gather_begin(1, pack(basis).astype(jnp.bfloat16))
    g01 = gram(probes, basis)
    g11 = gram(basis, basis)
    ar1[0, 0:64] = jnp.concatenate([g01, g11], axis=1)
    red = reduce_start(ar1, ar1r, 0)
    own = own_product(basis)
    state = gather_forward(1, state)
    reduce_finish(ar1, ar1r, 0, red)
    red = reduce_start(ar1, ar1r, 1)
    gather_across(1, state)
    gather_end_z(state)
    reduce_finish(ar1, ar1r, 1, red)
    red = reduce_start(ar1, ar1r, 2)
    forward_products(1)
    across = plane_begin(1)
    gather_end_plane(state)
    mirror_products(1)
    zs = z_begin(1)
    reduce_finish(ar1, ar1r, 2, red)
    red = reduce_start(ar1, ar1r, 3)
    mid = plane_stage(1, across)
    z_stage(1, zs)
    total = reduce_finish(ar1, ar1r, 3, red)
    g01, g11 = total[:, 0:Q], total[:, Q:]
    eye = (
        lax.broadcasted_iota(jnp.int32, (Q, Q), 0) == lax.broadcasted_iota(jnp.int32, (Q, Q), 1)
    ).astype(jnp.float32)
    alpha = solve(g01 + shift * rr0, rr0)
    m0 = eye - shift * alpha
    m1 = -alpha
    rr1 = (
        dot_hi(m0, dot_hi(rr0, m0, 1, 0) + dot_hi(g01, m1, 1, 0), 0, 0)
        + dot_hi(m1, dot_hi(g01, m0, 0, 0) + dot_hi(g11, m1, 1, 0), 0, 0)
    )
    beta = solve(rr0, rr1)
    n0 = m0 + beta
    last = plane_stage2(1, mid)
    residual = combine(m0, probes) + combine(m1, basis)
    direction = residual + combine(beta, probes)
    xsol = combine(alpha, probes)
    partial = combine(n0, image)
    deep = z_end(1, zs)
    deep = deep + plane_end(1, last)
    deep = own + unpack(deep)
    image2 = partial + combine(m1, deep)
    pq = gram(direction, image2)
    ar2[0, 0:32] = jnp.concatenate([pq[0:32], pq[32:64]], axis=1)
    for stage in range(4):
        red = reduce_start(ar2, ar2r, stage)
        total = reduce_finish(ar2, ar2r, stage, red)
    pq = jnp.concatenate([total[:, 0:Q], total[:, Q:]], axis=0)
    gamma = solve(pq, rr1)
    sol_ref[0] = xsol + combine(gamma, direction)
    res_ref[0] = residual - combine(gamma, image2)
    for copy in used:
        copy.wait_send()


def body(tiles, diag_tiles, probes, rows_list, cols_list, counts):
    smem = pl.BlockSpec(memory_space=pltpu.SMEM)
    vmem = pl.BlockSpec(memory_space=pltpu.VMEM)
    hbm = pl.BlockSpec(memory_space=pl.ANY)
    bf, f32, i32 = jnp.bfloat16, jnp.float32, jnp.int32
    return pl.pallas_call(
        kernel,
        out_shape=(jax.ShapeDtypeStruct((1, Q, B), f32),) * 2,
        in_specs=[smem, smem, smem, hbm, hbm, vmem],
        out_specs=(vmem, vmem),
        scratch_shapes=[
            pltpu.VMEM((SLOTS, B, B), bf),
            pltpu.VMEM((B, B), bf),
            pltpu.VMEM((2, 4, 4, PK, 128), bf),
            pltpu.VMEM((2, 4, 4, PK, 128), bf),
            pltpu.VMEM((ROWS, PK, 128), bf),
            pltpu.VMEM((ROWS, PK, 128), bf),
            pltpu.VMEM((2, 2, 4, 4, PK, 128), bf),
            pltpu.VMEM((2, 4, 4, PK, 128), bf),
            pltpu.VMEM((2, 2, 4, 4, HALF, 128), bf),
            pltpu.VMEM((2, 2, 3, 4, HALF, 128), bf),
            pltpu.VMEM((2, 2, 4, HALF, 128), bf),
            pltpu.VMEM((2, 2, 3, HALF, 128), bf),
            pltpu.VMEM((2, ROWS, PK, 128), bf),
            pltpu.VMEM((2, 2, PK, 128), bf),
            pltpu.VMEM((2, 2, PK, 128), bf),
            pltpu.VMEM((2, 2, HALF, 128), bf),
            pltpu.VMEM((2, 4, PK, 128), bf),
            pltpu.VMEM((SLOTS + 1, PK, 128), f32),
            pltpu.VMEM((SLOTS + 1, PK, 128), f32),
            pltpu.SMEM((SLOTS,), i32),
            pltpu.SMEM((SLOTS,), i32),
            pltpu.SMEM((PLANE,), i32),
            pltpu.SMEM((ROWS,), i32),
            pltpu.VMEM((4, 64, 128), f32),
            pltpu.VMEM((14, 64, 128), f32),
            pltpu.VMEM((4, 64, 128), f32),
            pltpu.VMEM((14, 64, 128), f32),
            pltpu.VMEM((4, 32, 128), f32),
            pltpu.VMEM((14, 32, 128), f32),
            pltpu.SemaphoreType.DMA((N_COPIES,)),
            pltpu.SemaphoreType.DMA((N_COPIES,)),
            pltpu.SemaphoreType.DMA((SLOTS,)),
            pltpu.SemaphoreType.DMA((1,)),
        ],
        compiler_params=pltpu.CompilerParams(
            collective_id=0, has_side_effects=True, vmem_limit_bytes=56 << 20
        ),
        name="block_cg",
    )(rows_list, cols_list, counts, tiles, diag_tiles, probes)


def solution(mesh):
    placed = (
        P("row", "col", None, None, None),
        P(("row", "col"), None, None),
        P(("row", "col"), None, None),
        P("row", "col", None),
        P("row", "col", None),
        P("row", "col"),
    )
    return jax.shard_map(
        body,
        mesh=mesh,
        in_specs=placed,
        out_specs=(P(("row", "col"), None, None), P(("row", "col"), None, None)),
        check_vma=False,
    )
```

```python
import jax
import jax.numpy as jnp
from jax import lax
from jax.experimental import pallas as pl
from jax.experimental.pallas import tpu as pltpu
from jax.sharding import PartitionSpec as P

MESH = pl.DeviceIdType.MESH
B, Q, SLOTS, ROWS, PLANE = 576, 64, 16, 8, 32
PK, HALF = 288, 144
STEPS = (1, 3, 2)
N_COPIES = 248
NT = 256
UNROLL = 4


def pack(v):
    tail = jnp.concatenate([v[0:32, 512:576], v[32:64, 512:576]], axis=1)
    return jnp.concatenate(
        [v[:, 0:128], v[:, 128:256], v[:, 256:384], v[:, 384:512], tail], axis=0
    )


def unpack(w):
    tail = jnp.concatenate([w[256:288, 0:64], w[256:288, 64:128]], axis=0)
    return jnp.concatenate(
        [w[0:64], w[64:128], w[128:192], w[192:256], tail], axis=1
    )


def dot(a, b, ca, cb):
    return lax.dot_general(
        a, b, (((ca,), (cb,)), ((), ())), preferred_element_type=jnp.float32
    )


def dot_hi(a, b, ca, cb):
    return lax.dot_general(
        a, b, (((ca,), (cb,)), ((), ())),
        precision=lax.Precision.HIGHEST, preferred_element_type=jnp.float32,
    )


def gram(a, b):
    return dot_hi(a, b, 1, 1)


def combine(coef, block):
    return dot_hi(coef, block, 0, 0)


def solve(matrix, rhs):
    i = lax.broadcasted_iota(jnp.int32, (Q, Q), 0)
    j = lax.broadcasted_iota(jnp.int32, (Q, Q), 1)
    sym = jnp.where(i >= j, matrix, matrix.T)
    work = jnp.concatenate([sym, rhs], axis=1)
    line = lax.broadcasted_iota(jnp.int32, (Q, 2 * Q), 0)
    n = 8
    for k in range(0, Q, n):
        col = [jnp.broadcast_to(work[:, k + a : k + a + 1], (Q, 2 * Q)) for a in range(n)]
        row = [work[k + a : k + a + 1, :] for a in range(n)]
        piv = [[col[b][k + a : k + a + 1, :] for b in range(n)] for a in range(n)]
        for a in range(n):
            inv = 1.0 / piv[a][a]
            row[a] = row[a] * inv
            for b in range(a + 1, n):
                piv[a][b] = piv[a][b] * inv
            for other in range(n):
                if other != a:
                    f = piv[other][a]
                    row[other] = row[other] - f * row[a]
                    for b in range(a + 1, n):
                        piv[other][b] = piv[other][b] - f * piv[a][b]
        new = work
        for a in range(n):
            new = new - col[a] * row[a]
        for a in range(n):
            new = jnp.where(line == k + a, row[a], new)
        work = new
    return work[:, Q:]


def fold(g):
    return jnp.concatenate([g[0:32], g[32:64]], axis=1)


def unfold(g):
    return jnp.concatenate([g[:, 0:Q], g[:, Q:]], axis=0)


def kernel(
    rows_ref, cols_ref, counts_ref, tiles_ref, diag_ref, probes_ref,
    sol_ref, res_ref,
    blocks, diag, rp_a, rp_b, cp_a, cp_b, ps, xb, qb, r1, sb, r2, pz, zq, zr1, zh, zr2,
    seg_r, seg_c, prev_r, prev_c, last_r, last_c,
    ar_a, ar_ar, ar_b, ar_br, ar_c, ar_cr, ar_d, ar_dr,
    send_sem, recv_sem, tile_sem, diag_sem,
):
    z = lax.axis_index("row")
    c = lax.axis_index("col")
    y, x, k = c // 8, (c // 2) % 4, c % 2

    def at(dz=0, dy=0, dx=0, flip=False):
        kk = 1 - k if flip else k
        return (
            lax.rem(z + dz + 8, 8),
            (lax.rem(y + dy + 4, 4) * 4 + lax.rem(x + dx + 4, 4)) * 2 + kk,
        )

    def wrap(v, n):
        return lax.rem(v + 2 * n, n)

    plane_of = {0: lambda d: at(dx=d), 1: lambda d: at(dy=d)}
    used = []
    rps, cps = (rp_a, rp_b), (cp_a, cp_b)

    def send(src, dst, device):
        i = len(used)
        copy = pltpu.make_async_remote_copy(
            src_ref=src, dst_ref=dst, send_sem=send_sem.at[i], recv_sem=recv_sem.at[i],
            device_id=device, device_id_type=MESH,
        )
        used.append(copy)
        copy.start()
        return copy

    tile_copies = [
        pltpu.make_async_copy(tiles_ref.at[0, 0, s], blocks.at[s], tile_sem.at[s])
        for s in range(SLOTS)
    ]
    diag_copy = pltpu.make_async_copy(diag_ref.at[0], diag, diag_sem.at[0])

    peers = [at(dx=d) for d in STEPS] + [at(dy=d) for d in STEPS]
    peers += [at(dz=d) for d in range(1, 8)] + [at(flip=True)]
    barrier = pltpu.get_barrier_semaphore()
    for peer in peers:
        pl.semaphore_signal(barrier, inc=1, device_id=peer, device_id_type=MESH)
    pl.semaphore_wait(barrier, len(peers))

    def half(h):
        return pl.ds(h * HALF, HALF)

    def gather_begin(p, value):
        rps[p][k, y, x] = value
        cps[p][z] = value
        first, second, far = [], [], []
        for h in range(2):
            own = rps[p].at[k, y, x, half(h)]
            first.append([send(own, own, plane_of[h](d)) for d in STEPS])
        own = cps[p].at[z]
        for d in (2, -2, 1, -1):
            far.append(send(own, own, at(dz=d)))
        for h in range(2):
            own = rps[p].at[k, y, x, half(h)]
            second.append([[send(own, own, plane_of[1 - h](e)) for e in STEPS]])
        return first, second, far

    def gather_forward(p, state):
        first, second, far = state
        for i, d in enumerate(STEPS):
            for h in range(2):
                first[h][i].wait_recv()
                ty, tx = (y, wrap(x - d, 4)) if h == 0 else (wrap(y - d, 4), x)
                got = rps[p].at[k, ty, tx, half(h)]
                second[h].append([send(got, got, plane_of[1 - h](e)) for e in STEPS])
        for i, d in enumerate((2, -2)):
            far[i].wait_recv()
            got = cps[p].at[wrap(z - d, 8)]
            far.append(send(got, got, at(dz=d // 2)))
            got = cps[p].at[wrap(z - d, 8), half(i)]
            far.append(send(got, got, at(dz=d)))
        third = []
        for h in range(2):
            group = rps[p].at[k, y, :, half(h)] if h == 0 else rps[p].at[k, :, x, half(h)]
            third.append(send(group, group, at(flip=True)))
        return first, second, far, third

    def gather_across(p, state):
        first, second, far, third = state
        for j, e in enumerate(STEPS):
            for h in range(2):
                for part in second[h]:
                    part[j].wait_recv()
                group = (
                    rps[p].at[k, wrap(y - e, 4), :, half(h)]
                    if h == 0
                    else rps[p].at[k, :, wrap(x - e, 4), half(h)]
                )
                third.append(send(group, group, at(flip=True)))

    def gather_end_z(state):
        far = state[2]
        for copy in far[2:]:
            copy.wait_recv()

    def gather_end_plane(state):
        for copy in state[3]:
            copy.wait_recv()

    def forward_products(p):
        def step(s, carry):
            far = unpack(cps[p][cols_ref[0, 0, s]])
            seg_r[s] = pack(dot(far, blocks[s], 1, 1)) + seg_r[prev_r[s]]
            return carry

        lax.fori_loop(0, SLOTS, step, 0, unroll=UNROLL)

    def mirror_products(p):
        count = counts_ref[0, 0]

        def step(s, cross):
            t = rows_ref[0, 0, s]
            near = unpack(rps[p][lax.rem(t, 2), t // 8, lax.rem(t // 2, 4)])
            far = unpack(cps[p][cols_ref[0, 0, s]])
            product = dot(near, blocks[s], 1, 0)
            seg_c[s] = pack(product) + seg_c[prev_c[s]]
            held = jnp.where(s < count, 1.0, 0.0)
            return cross + held * dot(far, product.astype(jnp.bfloat16), 1, 1)

        cross = lax.fori_loop(0, SLOTS, step, jnp.zeros((Q, Q), jnp.float32), unroll=UNROLL)
        return cross + cross.T

    def plane_begin(p):
        def fill(kk):
            @pl.loop(0, 16)
            def _(t):
                ps[p, kk, t // 4, lax.rem(t, 4)] = seg_r[last_r[2 * t + kk]].astype(jnp.bfloat16)

        fill(1 - k)
        out = []
        for d in (2, 1, 3, 0):
            for h in range(2):
                if h == 0:
                    t = wrap(x + d, 4)
                    src, dst = ps.at[p, 1 - k, :, t, half(h)], xb.at[p, :, t, half(h)]
                else:
                    t = wrap(y + d, 4)
                    src, dst = ps.at[p, 1 - k, t, :, half(h)], xb.at[p, t, :, half(h)]
                out.append(send(src, dst, at(flip=True)))
        fill(k)
        return out

    def plane_stage(p, across):
        out = [{}, {}]
        n = 0
        for d in (2, 1, 3, 0):
            for h in range(2):
                across[n].wait_recv()
                n += 1
                if h == 0:
                    t, mine = wrap(x + d, 4), y
                    total = ps[p, k, :, t, half(h)].astype(jnp.float32) + xb[p, :, t, half(h)].astype(jnp.float32)
                else:
                    t, mine = wrap(y + d, 4), x
                    total = ps[p, k, t, :, half(h)].astype(jnp.float32) + xb[p, t, :, half(h)].astype(jnp.float32)
                qb[p, h, d] = total.astype(jnp.bfloat16)
                out[h][d] = [
                    send(qb.at[p, h, d, wrap(mine + e, 4)], r1.at[p, h, d, e - 1], plane_of[1 - h](e))
                    for e in (2, 1, 3)
                ]
        return out

    def plane_stage2(p, mid):
        out = [[], []]
        for d in (2, 1, 3, 0):
            for h in range(2):
                for copy in mid[h][d]:
                    copy.wait_recv()
                total = qb[p, h, d, y if h == 0 else x].astype(jnp.float32)
                for e in range(3):
                    total = total + r1[p, h, d, e].astype(jnp.float32)
                if d != 0:
                    sb[p, h, d] = total.astype(jnp.bfloat16)
                    out[h].append(send(sb.at[p, h, d], r2.at[p, h, d - 1], plane_of[h](d)))
                else:
                    out[h].append(total)
        return out

    def plane_end(p, last):
        halves = []
        for h in range(2):
            total = last[h][3]
            for i, d in enumerate((2, 1, 3)):
                last[h][i].wait_recv()
                total = total + r2[p, h, d - 1].astype(jnp.float32)
            halves.append(total)
        return jnp.concatenate(halves, axis=0)

    def z_begin(p):
        @pl.loop(0, ROWS)
        def _(t):
            pz[p, t] = seg_c[last_c[t]].astype(jnp.bfloat16)

        out = [
            send(pz.at[p, wrap(z + 3, 8)], zr1.at[p, 0], at(dz=1)),
            send(pz.at[p, wrap(z - 3, 8)], zr1.at[p, 1], at(dz=-1)),
            send(pz.at[p, wrap(z + 4, 8), half(0)], zh.at[p, 0], at(dz=2)),
            send(pz.at[p, wrap(z + 4, 8), half(1)], zh.at[p, 1], at(dz=-2)),
            send(pz.at[p, wrap(z + 1, 8)], zr2.at[p, 0], at(dz=1)),
            send(pz.at[p, wrap(z - 1, 8)], zr2.at[p, 1], at(dz=-1)),
        ]
        return out

    def z_stage(p, out):
        for i, d in enumerate((2, -2)):
            out[i].wait_recv()
            out[2 + i].wait_recv()
            total = pz[p, wrap(z + d, 8)].astype(jnp.float32) + zr1[p, i].astype(jnp.float32)
            extra = zh[p, i].astype(jnp.float32)
            lo, hi = total[0:HALF], total[HALF:PK]
            if i == 0:
                lo = lo + extra
            else:
                hi = hi + extra
            zq[p, i, 0:HALF] = lo.astype(jnp.bfloat16)
            zq[p, i, HALF:PK] = hi.astype(jnp.bfloat16)
            out.append(send(zq.at[p, i], zr2.at[p, 2 + i], at(dz=d)))

    def z_end(p, out):
        total = pz[p, z].astype(jnp.float32)
        for i in range(4):
            out[4 + i].wait_recv()
            total = total + zr2[p, i].astype(jnp.float32)
        return total

    groups = (
        [at(flip=True)],
        [at(dx=d) for d in STEPS],
        [at(dy=d) for d in STEPS],
        [at(dz=d) for d in range(1, 8)],
    )
    bases = (0, 1, 4, 7)

    def reduce_steps(buf, rbuf, value):
        buf[0, 0 : value.shape[0]] = value
        for stage in range(4):
            copies = [
                send(buf.at[stage], rbuf.at[bases[stage] + i], peer)
                for i, peer in enumerate(groups[stage])
            ]
            yield None
            total = buf[stage]
            for i, copy in enumerate(copies):
                copy.wait_recv()
                total = total + rbuf[bases[stage] + i]
            if stage < 3:
                buf[stage + 1] = total
        yield total

    drained = [0]

    def drain():
        for copy in used[drained[0] :]:
            copy.wait_send()
        drained[0] = len(used)

    def own_product(v):
        hi = v.astype(jnp.bfloat16)
        lo = (v - hi.astype(jnp.float32)).astype(jnp.bfloat16)
        d = diag[...]
        return dot(hi, d, 1, 1) + dot(lo, d, 1, 1)

    probes = probes_ref[0]
    state = gather_begin(0, pack(probes).astype(jnp.bfloat16))
    diag_copy.start()
    for copy in tile_copies[:8]:
        copy.start()

    count = counts_ref[0, 0]
    for s in range(SLOTS):
        pr = jnp.int32(SLOTS)
        pc = jnp.int32(SLOTS)
        for u in range(s):
            pr = jnp.where(rows_ref[0, 0, u] == rows_ref[0, 0, s], u, pr)
            pc = jnp.where(cols_ref[0, 0, u] == cols_ref[0, 0, s], u, pc)
        prev_r[s] = pr
        prev_c[s] = pc

    @pl.loop(0, PLANE)
    def _(t):
        at_slot = jnp.int32(SLOTS)
        for s in range(SLOTS):
            at_slot = jnp.where((rows_ref[0, 0, s] == t) & (s < count), s, at_slot)
        last_r[t] = at_slot

    @pl.loop(0, ROWS)
    def _(t):
        at_slot = jnp.int32(SLOTS)
        for s in range(SLOTS):
            at_slot = jnp.where((cols_ref[0, 0, s] == t) & (s < count), s, at_slot)
        last_c[t] = at_slot

    seg_r[SLOTS] = jnp.zeros((PK, 128), jnp.float32)
    seg_c[SLOTS] = jnp.zeros((PK, 128), jnp.float32)

    g00 = gram(probes, probes)
    diag_copy.wait()
    trace = jnp.zeros((1, 1), jnp.float32)
    for j in range(5):
        n = 128 if j < 4 else 64
        d = diag[pl.ds(128 * j, n), pl.ds(128 * j, n)].astype(jnp.float32)
        on = lax.broadcasted_iota(jnp.int32, (n, n), 0) == lax.broadcasted_iota(jnp.int32, (n, n), 1)
        trace = trace + jnp.sum(jnp.where(on, d, 0.0), keepdims=True)
    red_a = reduce_steps(
        ar_a, ar_ar, jnp.concatenate([fold(g00), jnp.broadcast_to(trace, (8, 128))], axis=0)
    )
    next(red_a)
    state = gather_forward(0, state)
    for copy in tile_copies[8:]:
        copy.start()
    next(red_a)
    own = own_product(probes)
    gather_across(0, state)
    next(red_a)
    gather_end_z(state)
    for copy in tile_copies:
        copy.wait()
    forward_products(0)
    across = plane_begin(0)
    next(red_a)
    gather_end_plane(state)
    cross = mirror_products(0)
    zs = z_begin(0)
    red_b = reduce_steps(ar_b, ar_br, fold(gram(probes, own) + cross))
    next(red_b)
    mid = plane_stage(0, across)
    total = next(red_a)
    rr0 = unfold(total[0:32])
    shift = total[32:33, 0:1] * (1.0 / (NT * B))
    z_stage(0, zs)
    next(red_b)
    eye = (
        lax.broadcasted_iota(jnp.int32, (Q, Q), 0) == lax.broadcasted_iota(jnp.int32, (Q, Q), 1)
    ).astype(jnp.float32)
    rr0_inv = solve(rr0, eye)
    last = plane_stage2(0, mid)
    next(red_b)
    image = z_end(0, zs)
    image = image + plane_end(0, last)
    image = own + unpack(image)
    basis = image - shift * probes

    state = gather_begin(1, pack(basis).astype(jnp.bfloat16))
    next(red_b)
    red_c = reduce_steps(ar_c, ar_cr, fold(gram(basis, basis)))
    next(red_c)
    own = own_product(basis)
    state = gather_forward(1, state)
    next(red_c)
    pq0 = unfold(next(red_b))
    alpha = solve(pq0, rr0)
    drain()
    gather_across(1, state)
    next(red_c)
    gather_end_z(state)
    forward_products(1)
    across = plane_begin(1)
    next(red_c)
    gather_end_plane(state)
    cross = mirror_products(1)
    zs = z_begin(1)
    red_d = reduce_steps(ar_d, ar_dr, fold(gram(basis, own) + cross))
    next(red_d)
    mid = plane_stage(1, across)
    g11 = unfold(next(red_c))
    g01 = pq0 - shift * rr0
    m0 = eye - shift * alpha
    m1 = -alpha
    rr1 = (
        dot_hi(m0, dot_hi(rr0, m0, 1, 0) + dot_hi(g01, m1, 1, 0), 0, 0)
        + dot_hi(m1, dot_hi(g01, m0, 0, 0) + dot_hi(g11, m1, 1, 0), 0, 0)
    )
    beta = dot_hi(rr0_inv, rr1, 1, 0)
    n0 = m0 + beta
    z_stage(1, zs)
    next(red_d)
    residual = combine(m0, probes) + combine(m1, basis)
    direction = residual + combine(beta, probes)
    xsol = combine(alpha, probes)
    partial = combine(n0, image)
    next(red_d)
    last = plane_stage2(1, mid)
    next(red_d)
    g12 = unfold(next(red_d))
    g02 = g11 + shift * g01
    pq1 = (
        dot_hi(n0, dot_hi(pq0, n0, 1, 0) + dot_hi(g02, m1, 1, 0), 0, 0)
        + dot_hi(m1, dot_hi(g02, n0, 0, 0) + dot_hi(g12, m1, 1, 0), 0, 0)
    )
    gamma = solve(pq1, rr1)
    sol_ref[0] = xsol + combine(gamma, direction)
    start = residual - combine(gamma, partial)
    m2 = dot_hi(m1, gamma, 1, 0)
    deep = z_end(1, zs)
    deep = deep + plane_end(1, last)
    deep = own + unpack(deep)
    res_ref[0] = start - combine(m2, deep)
    drain()


def body(tiles, diag_tiles, probes, rows_list, cols_list, counts):
    smem = pl.BlockSpec(memory_space=pltpu.SMEM)
    vmem = pl.BlockSpec(memory_space=pltpu.VMEM)
    hbm = pl.BlockSpec(memory_space=pl.ANY)
    bf, f32, i32 = jnp.bfloat16, jnp.float32, jnp.int32
    return pl.pallas_call(
        kernel,
        out_shape=(jax.ShapeDtypeStruct((1, Q, B), f32),) * 2,
        in_specs=[smem, smem, smem, hbm, hbm, vmem],
        out_specs=(vmem, vmem),
        scratch_shapes=[
            pltpu.VMEM((SLOTS, B, B), bf),
            pltpu.VMEM((B, B), bf),
            pltpu.VMEM((2, 4, 4, PK, 128), bf),
            pltpu.VMEM((2, 4, 4, PK, 128), bf),
            pltpu.VMEM((ROWS, PK, 128), bf),
            pltpu.VMEM((ROWS, PK, 128), bf),
            pltpu.VMEM((2, 2, 4, 4, PK, 128), bf),
            pltpu.VMEM((2, 4, 4, PK, 128), bf),
            pltpu.VMEM((2, 2, 4, 4, HALF, 128), bf),
            pltpu.VMEM((2, 2, 4, 3, HALF, 128), bf),
            pltpu.VMEM((2, 2, 4, HALF, 128), bf),
            pltpu.VMEM((2, 2, 3, HALF, 128), bf),
            pltpu.VMEM((2, ROWS, PK, 128), bf),
            pltpu.VMEM((2, 2, PK, 128), bf),
            pltpu.VMEM((2, 2, PK, 128), bf),
            pltpu.VMEM((2, 2, HALF, 128), bf),
            pltpu.VMEM((2, 4, PK, 128), bf),
            pltpu.VMEM((SLOTS + 1, PK, 128), f32),
            pltpu.VMEM((SLOTS + 1, PK, 128), f32),
            pltpu.SMEM((SLOTS,), i32),
            pltpu.SMEM((SLOTS,), i32),
            pltpu.SMEM((PLANE,), i32),
            pltpu.SMEM((ROWS,), i32),
            pltpu.VMEM((4, 40, 128), f32),
            pltpu.VMEM((14, 40, 128), f32),
            pltpu.VMEM((4, 32, 128), f32),
            pltpu.VMEM((14, 32, 128), f32),
            pltpu.VMEM((4, 32, 128), f32),
            pltpu.VMEM((14, 32, 128), f32),
            pltpu.VMEM((4, 32, 128), f32),
            pltpu.VMEM((14, 32, 128), f32),
            pltpu.SemaphoreType.DMA((N_COPIES,)),
            pltpu.SemaphoreType.DMA((N_COPIES,)),
            pltpu.SemaphoreType.DMA((SLOTS,)),
            pltpu.SemaphoreType.DMA((1,)),
        ],
        compiler_params=pltpu.CompilerParams(
            collective_id=0, has_side_effects=True, vmem_limit_bytes=56 << 20
        ),
        name="block_cg",
    )(rows_list, cols_list, counts, tiles, diag_tiles, probes)


def solution(mesh):
    placed = (
        P("row", "col", None, None, None),
        P(("row", "col"), None, None),
        P(("row", "col"), None, None),
        P("row", "col", None),
        P("row", "col", None),
        P("row", "col"),
    )
    return jax.shard_map(
        body,
        mesh=mesh,
        in_specs=placed,
        out_specs=(P(("row", "col"), None, None), P(("row", "col"), None, None)),
        check_vma=False,
    )
```

```python
import math

import jax
import jax.numpy as jnp
from jax import lax
from jax.experimental import pallas as pl
from jax.experimental.pallas import tpu as pltpu
from jax.sharding import PartitionSpec as P

MESH = pl.DeviceIdType.MESH
B, Q, SLOTS, ROWS, PLANE = 576, 64, 16, 8, 32
PK, HALF = 288, 144
STEPS = (1, 3, 2)
ORDER = (2, 1, 3, 0)
N_ARRIVALS = 92
SENT = 26000
NT = 256
UNROLL = 4


def pack(v):
    tail = jnp.concatenate([v[0:32, 512:576], v[32:64, 512:576]], axis=1)
    return jnp.concatenate(
        [v[:, 0:128], v[:, 128:256], v[:, 256:384], v[:, 384:512], tail], axis=0
    )


def unpack(w):
    tail = jnp.concatenate([w[256:288, 0:64], w[256:288, 64:128]], axis=0)
    return jnp.concatenate(
        [w[0:64], w[64:128], w[128:192], w[192:256], tail], axis=1
    )


def dot(a, b, ca, cb):
    return lax.dot_general(
        a, b, (((ca,), (cb,)), ((), ())), preferred_element_type=jnp.float32
    )


def dot_hi(a, b, ca, cb):
    return lax.dot_general(
        a, b, (((ca,), (cb,)), ((), ())),
        precision=lax.Precision.HIGHEST, preferred_element_type=jnp.float32,
    )


def gram(a, b):
    return dot_hi(a, b, 1, 1)


def combine(coef, block):
    return dot_hi(coef, block, 0, 0)


def solve(matrix, rhs):
    i = lax.broadcasted_iota(jnp.int32, (Q, Q), 0)
    j = lax.broadcasted_iota(jnp.int32, (Q, Q), 1)
    sym = jnp.where(i >= j, matrix, matrix.T)
    work = jnp.concatenate([sym, rhs], axis=1)
    line = lax.broadcasted_iota(jnp.int32, (Q, 2 * Q), 0)
    n = 8
    for k in range(0, Q, n):
        col = [jnp.broadcast_to(work[:, k + a : k + a + 1], (Q, 2 * Q)) for a in range(n)]
        row = [work[k + a : k + a + 1, :] for a in range(n)]
        piv = [[col[b][k + a : k + a + 1, :] for b in range(n)] for a in range(n)]
        for a in range(n):
            inv = 1.0 / piv[a][a]
            row[a] = row[a] * inv
            for b in range(a + 1, n):
                piv[a][b] = piv[a][b] * inv
            for other in range(n):
                if other != a:
                    f = piv[other][a]
                    row[other] = row[other] - f * row[a]
                    for b in range(a + 1, n):
                        piv[other][b] = piv[other][b] - f * piv[a][b]
        new = work
        for a in range(n):
            new = new - col[a] * row[a]
        for a in range(n):
            new = jnp.where(line == k + a, row[a], new)
        work = new
    return work[:, Q:]


def fold(g):
    return jnp.concatenate([g[0:32], g[32:64]], axis=1)


def unfold(g):
    return jnp.concatenate([g[:, 0:Q], g[:, Q:]], axis=0)


def kernel(
    rows_ref, cols_ref, counts_ref, tiles_ref, diag_ref, probes_ref,
    sol_ref, res_ref,
    blocks, diag, rp_a, rp_b, cp_a, cp_b, ps, xb, qb, r1, sb, r2, pz, zq, zin, zr2, gone,
    seg_r, seg_c, prev_r, prev_c, last_r, last_c,
    ar_a, ar_ar, ar_b, ar_br, ar_c, ar_cr, ar_d, ar_dr,
    send_sem, recv_sem, tile_sem, diag_sem,
):
    z = lax.axis_index("row")
    c = lax.axis_index("col")
    y, x, k = c // 8, (c // 2) % 4, c % 2

    def at(dz=0, dy=0, dx=0, flip=False):
        kk = 1 - k if flip else k
        return (
            lax.rem(z + dz + 8, 8),
            (lax.rem(y + dy + 4, 4) * 4 + lax.rem(x + dx + 4, 4)) * 2 + kk,
        )

    def wrap(v, n):
        return lax.rem(v + 2 * n, n)

    plane_of = {0: lambda d: at(dx=d), 1: lambda d: at(dy=d)}
    rps, cps = (rp_a, rp_b), (cp_a, cp_b)
    arrivals = [0]
    sent = [0, 0]
    turn = [0]

    def group():
        arrivals[0] += 1
        return arrivals[0] - 1

    def send(src, dst, device, g):
        pltpu.make_async_remote_copy(
            src_ref=src, dst_ref=dst, send_sem=send_sem.at[turn[0]], recv_sem=recv_sem.at[g],
            device_id=device, device_id_type=MESH,
        ).start()
        width = 1 if src.dtype == jnp.bfloat16 else 2
        sent[turn[0]] += width * math.prod(src.shape) // 128

    def take(g, ref):
        pltpu.make_async_remote_copy(
            src_ref=ref, dst_ref=ref, send_sem=send_sem.at[0], recv_sem=recv_sem.at[g],
            device_id=at(flip=True), device_id_type=MESH,
        ).wait_recv()

    def drain(p):
        ref = gone.at[pl.ds(0, sent[p])]
        pltpu.make_async_remote_copy(
            src_ref=ref, dst_ref=ref, send_sem=send_sem.at[p], recv_sem=recv_sem.at[0],
            device_id=at(flip=True), device_id_type=MESH,
        ).wait_send()

    tile_copies = [
        pltpu.make_async_copy(tiles_ref.at[0, 0, s], blocks.at[s], tile_sem.at[0])
        for s in range(SLOTS)
    ]
    diag_copy = pltpu.make_async_copy(diag_ref.at[0], diag, diag_sem.at[0])

    peers = [at(dx=d) for d in STEPS] + [at(dy=d) for d in STEPS]
    peers += [at(dz=d) for d in range(1, 8)] + [at(flip=True)]
    barrier = pltpu.get_barrier_semaphore()
    for peer in peers:
        pl.semaphore_signal(barrier, inc=1, device_id=peer, device_id_type=MESH)
    pl.semaphore_wait(barrier, len(peers))

    def half(h):
        return pl.ds(h * HALF, HALF)

    def gather_begin(p, value):
        rps[p][k, y, x] = value
        cps[p][z] = value
        first = [[group() for _ in STEPS] for _ in range(2)]
        second = [[group() for _ in STEPS] for _ in range(2)]
        far, rest, across = [group(), group()], group(), group()
        own = cps[p].at[z]
        for d, g in ((2, far[0]), (-2, far[1])):
            send(own, own, at(dz=d), g)
        for i, d in enumerate(STEPS):
            for h in range(2):
                own = rps[p].at[k, y, x, half(h)]
                send(own, own, plane_of[h](d), first[h][i])
        own = cps[p].at[z]
        for d in (1, -1):
            send(own, own, at(dz=d), rest)
        for j, e in enumerate(STEPS):
            for h in range(2):
                own = rps[p].at[k, y, x, half(h)]
                send(own, own, plane_of[1 - h](e), second[h][j])
        return first, second, far, rest, across

    def gather_forward(p, state):
        first, second, far, rest, across = state
        for i, d in enumerate(STEPS):
            for h in range(2):
                ty, tx = (y, wrap(x - d, 4)) if h == 0 else (wrap(y - d, 4), x)
                got = rps[p].at[k, ty, tx, half(h)]
                take(first[h][i], got)
                for j, e in enumerate(STEPS):
                    send(got, got, plane_of[1 - h](e), second[h][j])
        for i, d in enumerate((2, -2)):
            got = cps[p].at[wrap(z - d, 8)]
            take(far[i], got)
            send(got, got, at(dz=d // 2), rest)
            got = cps[p].at[wrap(z - d, 8), half(i)]
            send(got, got, at(dz=d), rest)
        for h in range(2):
            line = rps[p].at[k, y, :, half(h)] if h == 0 else rps[p].at[k, :, x, half(h)]
            send(line, line, at(flip=True), across)

    def gather_across(p, state):
        first, second, far, rest, across = state
        for j, e in enumerate(STEPS):
            for h in range(2):
                line = (
                    rps[p].at[k, wrap(y - e, 4), :, half(h)]
                    if h == 0
                    else rps[p].at[k, :, wrap(x - e, 4), half(h)]
                )
                take(second[h][j], line)
                send(line, line, at(flip=True), across)

    def gather_end_z(p, state):
        take(state[3], cps[p].at[pl.ds(0, 5)])

    def gather_end_plane(p, state):
        take(state[4], rps[p].at[1 - k])

    def forward_products(p):
        def step(s, carry):
            far = unpack(cps[p][cols_ref[0, 0, s]])
            seg_r[s] = pack(dot(far, blocks[s], 1, 1)) + seg_r[prev_r[s]]
            return carry

        lax.fori_loop(0, SLOTS, step, 0, unroll=UNROLL)

    def mirror_products(p, low, high, cross):
        count = counts_ref[0, 0]

        def step(s, cross):
            t = rows_ref[0, 0, s]
            near = unpack(rps[p][lax.rem(t, 2), t // 8, lax.rem(t // 2, 4)])
            far = unpack(cps[p][cols_ref[0, 0, s]])
            product = dot(near, blocks[s], 1, 0)
            seg_c[s] = pack(product) + seg_c[prev_c[s]]
            held = jnp.where(s < count, 1.0, 0.0)
            return cross + held * dot(far, product.astype(jnp.bfloat16), 1, 1)

        return lax.fori_loop(low, high, step, cross, unroll=UNROLL)

    def plane_begin(p):
        def fill(kk):
            @pl.loop(0, 16)
            def _(t):
                ps[p, kk, t // 4, lax.rem(t, 4)] = seg_r[last_r[2 * t + kk]].astype(jnp.bfloat16)

        fill(1 - k)
        across = {}
        for d in ORDER:
            for h in range(2):
                across[h, d] = group()
                if h == 0:
                    t = wrap(x + d, 4)
                    src, dst = ps.at[p, 1 - k, :, t, half(h)], xb.at[p, :, t, half(h)]
                else:
                    t = wrap(y + d, 4)
                    src, dst = ps.at[p, 1 - k, t, :, half(h)], xb.at[p, t, :, half(h)]
                send(src, dst, at(flip=True), across[h, d])
        fill(k)
        return across

    def plane_stage(p, across, d):
        out = []
        for h in range(2):
            if h == 0:
                t, mine = wrap(x + d, 4), y
                take(across[h, d], xb.at[p, :, t, half(h)])
                total = ps[p, k, :, t, half(h)].astype(jnp.float32) + xb[p, :, t, half(h)].astype(jnp.float32)
            else:
                t, mine = wrap(y + d, 4), x
                take(across[h, d], xb.at[p, t, :, half(h)])
                total = ps[p, k, t, :, half(h)].astype(jnp.float32) + xb[p, t, :, half(h)].astype(jnp.float32)
            qb[p, h, d] = total.astype(jnp.bfloat16)
            g = group()
            for e in (2, 1, 3):
                send(qb.at[p, h, d, wrap(mine + e, 4)], r1.at[p, h, d, e - 1], plane_of[1 - h](e), g)
            out.append(g)
        return out

    def plane_stage2(p, mid, hooks):
        last = group()
        own = []
        for d in ORDER:
            for h in range(2):
                take(mid[d][h], r1.at[p, h, d])
                total = qb[p, h, d, y if h == 0 else x].astype(jnp.float32)
                for e in range(3):
                    total = total + r1[p, h, d, e].astype(jnp.float32)
                if d != 0:
                    sb[p, h, d] = total.astype(jnp.bfloat16)
                    send(sb.at[p, h, d], r2.at[p, h, d - 1], plane_of[h](d), last)
                else:
                    own.append(total)
            if d in hooks:
                hooks[d]()
        return last, own

    def plane_end(p, state):
        last, own = state
        take(last, r2.at[p])
        halves = []
        for h in range(2):
            total = own[h]
            for d in range(3):
                total = total + r2[p, h, d].astype(jnp.float32)
            halves.append(total)
        return jnp.concatenate(halves, axis=0)

    def z_begin(p):
        @pl.loop(0, ROWS)
        def _(t):
            pz[p, t] = seg_c[last_c[t]].astype(jnp.bfloat16)

        near, far = [group(), group()], group()
        for i, d in enumerate((1, -1)):
            send(pz.at[p, wrap(z + 3 * d, 8)], zin.at[p, i, pl.ds(0, PK)], at(dz=d), near[i])
            send(pz.at[p, wrap(z + 4, 8), half(i)], zin.at[p, i, pl.ds(PK, HALF)], at(dz=2 * d), near[i])
        for i, d in enumerate((1, -1)):
            send(pz.at[p, wrap(z + d, 8)], zr2.at[p, i], at(dz=d), far)
        return near, far

    def z_stage(p, state):
        near, far = state
        for i, d in enumerate((2, -2)):
            take(near[i], zin.at[p, i])
            total = pz[p, wrap(z + d, 8)].astype(jnp.float32) + zin[p, i, 0:PK].astype(jnp.float32)
            extra = zin[p, i, PK : PK + HALF].astype(jnp.float32)
            lo, hi = total[0:HALF], total[HALF:PK]
            if i == 0:
                lo = lo + extra
            else:
                hi = hi + extra
            zq[p, i, 0:HALF] = lo.astype(jnp.bfloat16)
            zq[p, i, HALF:PK] = hi.astype(jnp.bfloat16)
            send(zq.at[p, i], zr2.at[p, 2 + i], at(dz=d), far)

    def z_end(p, state):
        take(state[1], zr2.at[p])
        total = pz[p, z].astype(jnp.float32)
        for i in range(4):
            total = total + zr2[p, i].astype(jnp.float32)
        return total

    groups = (
        [at(flip=True)],
        [at(dx=d) for d in STEPS],
        [at(dy=d) for d in STEPS],
        [at(dz=d) for d in range(1, 8)],
    )
    bases = (0, 1, 4, 7)

    def reduce_steps(buf, rbuf, value):
        buf[0] = value
        for stage in range(4):
            g = group()
            for i, peer in enumerate(groups[stage]):
                send(buf.at[stage], rbuf.at[bases[stage] + i], peer, g)
            yield None
            total = buf[stage]
            n = len(groups[stage])
            take(g, rbuf.at[pl.ds(bases[stage], n)])
            for i in range(n):
                total = total + rbuf[bases[stage] + i]
            if stage < 3:
                buf[stage + 1] = total
        yield total

    def own_product(v):
        hi = v.astype(jnp.bfloat16)
        lo = (v - hi.astype(jnp.float32)).astype(jnp.bfloat16)
        d = diag[...]
        return dot(hi, d, 1, 1) + dot(lo, d, 1, 1)

    probes = probes_ref[0]
    state = gather_begin(0, pack(probes).astype(jnp.bfloat16))
    diag_copy.start()
    for copy in tile_copies[:8]:
        copy.start()

    count = counts_ref[0, 0]
    for s in range(SLOTS):
        pr = jnp.int32(SLOTS)
        pc = jnp.int32(SLOTS)
        for u in range(s):
            pr = jnp.where(rows_ref[0, 0, u] == rows_ref[0, 0, s], u, pr)
            pc = jnp.where(cols_ref[0, 0, u] == cols_ref[0, 0, s], u, pc)
        prev_r[s] = pr
        prev_c[s] = pc

    @pl.loop(0, PLANE)
    def _(t):
        at_slot = jnp.int32(SLOTS)
        for s in range(SLOTS):
            at_slot = jnp.where((rows_ref[0, 0, s] == t) & (s < count), s, at_slot)
        last_r[t] = at_slot

    @pl.loop(0, ROWS)
    def _(t):
        at_slot = jnp.int32(SLOTS)
        for s in range(SLOTS):
            at_slot = jnp.where((cols_ref[0, 0, s] == t) & (s < count), s, at_slot)
        last_c[t] = at_slot

    seg_r[SLOTS] = jnp.zeros((PK, 128), jnp.float32)
    seg_c[SLOTS] = jnp.zeros((PK, 128), jnp.float32)

    g00 = gram(probes, probes)
    diag_copy.wait()
    trace = jnp.zeros((1, 1), jnp.float32)
    for j in range(5):
        n = 128 if j < 4 else 64
        d = diag[pl.ds(128 * j, n), pl.ds(128 * j, n)].astype(jnp.float32)
        on = lax.broadcasted_iota(jnp.int32, (n, n), 0) == lax.broadcasted_iota(jnp.int32, (n, n), 1)
        trace = trace + jnp.sum(jnp.where(on, d, 0.0), keepdims=True)
    red_a = reduce_steps(
        ar_a, ar_ar, jnp.concatenate([fold(g00), jnp.broadcast_to(trace, (8, 128))], axis=0)
    )
    next(red_a)
    gather_forward(0, state)
    for copy in tile_copies[8:]:
        copy.start()
    next(red_a)
    own = own_product(probes)
    gather_across(0, state)
    next(red_a)
    gather_end_z(0, state)
    pltpu.make_async_copy(tiles_ref.at[0, 0], blocks, tile_sem.at[0]).wait()
    forward_products(0)
    across = plane_begin(0)
    next(red_a)
    gather_end_plane(0, state)
    mid = {}
    cross = mirror_products(0, 0, 8, jnp.zeros((Q, Q), jnp.float32))
    mid[2] = plane_stage(0, across, 2)
    cross = mirror_products(0, 8, 12, cross)
    mid[1] = plane_stage(0, across, 1)
    cross = mirror_products(0, 12, 16, cross)
    cross = cross + cross.T
    zs = z_begin(0)
    mid[3] = plane_stage(0, across, 3)
    mid[0] = plane_stage(0, across, 0)
    red_b = reduce_steps(ar_b, ar_br, fold(gram(probes, own) + cross))
    next(red_b)
    total = next(red_a)
    rr0 = unfold(total[0:32])
    shift = total[32:33, 0:1] * (1.0 / (NT * B))
    eye = (
        lax.broadcasted_iota(jnp.int32, (Q, Q), 0) == lax.broadcasted_iota(jnp.int32, (Q, Q), 1)
    ).astype(jnp.float32)
    rr0_inv = solve(rr0, eye)
    next(red_b)
    z_stage(0, zs)
    last = plane_stage2(0, mid, {2: lambda: next(red_b), 3: lambda: next(red_b)})
    image = z_end(0, zs)
    image = image + plane_end(0, last)
    image = own + unpack(image)
    basis = image - shift * probes

    turn[0] = 1
    state = gather_begin(1, pack(basis).astype(jnp.bfloat16))
    red_c = reduce_steps(ar_c, ar_cr, fold(gram(basis, basis)))
    next(red_c)
    own = own_product(basis)
    gather_forward(1, state)
    next(red_c)
    pq0 = unfold(next(red_b))
    alpha = solve(pq0, rr0)
    drain(0)
    gather_across(1, state)
    next(red_c)
    gather_end_z(1, state)
    forward_products(1)
    across = plane_begin(1)
    next(red_c)
    gather_end_plane(1, state)
    mid = {}
    cross = mirror_products(1, 0, 8, jnp.zeros((Q, Q), jnp.float32))
    mid[2] = plane_stage(1, across, 2)
    cross = mirror_products(1, 8, 12, cross)
    mid[1] = plane_stage(1, across, 1)
    cross = mirror_products(1, 12, 16, cross)
    cross = cross + cross.T
    zs = z_begin(1)
    red_d = reduce_steps(ar_d, ar_dr, fold(gram(basis, own) + cross))
    next(red_d)
    mid[3] = plane_stage(1, across, 3)
    mid[0] = plane_stage(1, across, 0)
    next(red_d)
    g11 = unfold(next(red_c))
    g01 = pq0 - shift * rr0
    m0 = eye - shift * alpha
    m1 = -alpha
    rr1 = (
        dot_hi(m0, dot_hi(rr0, m0, 1, 0) + dot_hi(g01, m1, 1, 0), 0, 0)
        + dot_hi(m1, dot_hi(g01, m0, 0, 0) + dot_hi(g11, m1, 1, 0), 0, 0)
    )
    beta = dot_hi(rr0_inv, rr1, 1, 0)
    n0 = m0 + beta
    residual = combine(m0, probes) + combine(m1, basis)
    next(red_d)
    z_stage(1, zs)
    direction = residual + combine(beta, probes)
    xsol = combine(alpha, probes)
    partial = combine(n0, image)
    final = []
    last = plane_stage2(1, mid, {2: lambda: next(red_d), 0: lambda: final.append(next(red_d))})
    g12 = unfold(final[0])
    g02 = g11 + shift * g01
    pq1 = (
        dot_hi(n0, dot_hi(pq0, n0, 1, 0) + dot_hi(g02, m1, 1, 0), 0, 0)
        + dot_hi(m1, dot_hi(g02, n0, 0, 0) + dot_hi(g12, m1, 1, 0), 0, 0)
    )
    gamma = solve(pq1, rr1)
    sol_ref[0] = xsol + combine(gamma, direction)
    start = residual - combine(gamma, partial)
    m2 = dot_hi(m1, gamma, 1, 0)
    deep = z_end(1, zs)
    deep = deep + plane_end(1, last)
    deep = own + unpack(deep)
    res_ref[0] = start - combine(m2, deep)
    drain(1)


def body(tiles, diag_tiles, probes, rows_list, cols_list, counts):
    smem = pl.BlockSpec(memory_space=pltpu.SMEM)
    vmem = pl.BlockSpec(memory_space=pltpu.VMEM)
    hbm = pl.BlockSpec(memory_space=pl.ANY)
    bf, f32, i32 = jnp.bfloat16, jnp.float32, jnp.int32
    return pl.pallas_call(
        kernel,
        out_shape=(jax.ShapeDtypeStruct((1, Q, B), f32),) * 2,
        in_specs=[smem, smem, smem, hbm, hbm, vmem],
        out_specs=(vmem, vmem),
        scratch_shapes=[
            pltpu.VMEM((SLOTS, B, B), bf),
            pltpu.VMEM((B, B), bf),
            pltpu.VMEM((2, 4, 4, PK, 128), bf),
            pltpu.VMEM((2, 4, 4, PK, 128), bf),
            pltpu.VMEM((ROWS, PK, 128), bf),
            pltpu.VMEM((ROWS, PK, 128), bf),
            pltpu.VMEM((2, 2, 4, 4, PK, 128), bf),
            pltpu.VMEM((2, 4, 4, PK, 128), bf),
            pltpu.VMEM((2, 2, 4, 4, HALF, 128), bf),
            pltpu.VMEM((2, 2, 4, 3, HALF, 128), bf),
            pltpu.VMEM((2, 2, 4, HALF, 128), bf),
            pltpu.VMEM((2, 2, 3, HALF, 128), bf),
            pltpu.VMEM((2, ROWS, PK, 128), bf),
            pltpu.VMEM((2, 2, PK, 128), bf),
            pltpu.VMEM((2, 2, PK + HALF, 128), bf),
            pltpu.VMEM((2, 4, PK, 128), bf),
            pltpu.VMEM((SENT, 128), bf),
            pltpu.VMEM((SLOTS + 1, PK, 128), f32),
            pltpu.VMEM((SLOTS + 1, PK, 128), f32),
            pltpu.SMEM((SLOTS,), i32),
            pltpu.SMEM((SLOTS,), i32),
            pltpu.SMEM((PLANE,), i32),
            pltpu.SMEM((ROWS,), i32),
            pltpu.VMEM((4, 40, 128), f32),
            pltpu.VMEM((14, 40, 128), f32),
            pltpu.VMEM((4, 32, 128), f32),
            pltpu.VMEM((14, 32, 128), f32),
            pltpu.VMEM((4, 32, 128), f32),
            pltpu.VMEM((14, 32, 128), f32),
            pltpu.VMEM((4, 32, 128), f32),
            pltpu.VMEM((14, 32, 128), f32),
            pltpu.SemaphoreType.DMA((2,)),
            pltpu.SemaphoreType.DMA((N_ARRIVALS,)),
            pltpu.SemaphoreType.DMA((1,)),
            pltpu.SemaphoreType.DMA((1,)),
        ],
        compiler_params=pltpu.CompilerParams(
            collective_id=0, has_side_effects=True, vmem_limit_bytes=56 << 20
        ),
        name="block_cg",
    )(rows_list, cols_list, counts, tiles, diag_tiles, probes)


def solution(mesh):
    placed = (
        P("row", "col", None, None, None),
        P(("row", "col"), None, None),
        P(("row", "col"), None, None),
        P("row", "col", None),
        P("row", "col", None),
        P("row", "col"),
    )
    return jax.shard_map(
        body,
        mesh=mesh,
        in_specs=placed,
        out_specs=(P(("row", "col"), None, None), P(("row", "col"), None, None)),
        check_vma=False,
    )
```

```python
import math

import jax
import jax.numpy as jnp
from jax import lax
from jax.experimental import pallas as pl
from jax.experimental.pallas import tpu as pltpu
from jax.sharding import PartitionSpec as P

MESH = pl.DeviceIdType.MESH
B, Q, SLOTS, ROWS, PLANE = 576, 64, 16, 8, 32
PK, HALF = 288, 144
STEPS = (1, 3, 2)
ORDER = (2, 1, 3, 0)
N_ARRIVALS = 92
SENT = 26000
NT = 256
UNROLL = 4


def pack(v):
    tail = jnp.concatenate([v[0:32, 512:576], v[32:64, 512:576]], axis=1)
    return jnp.concatenate(
        [v[:, 0:128], v[:, 128:256], v[:, 256:384], v[:, 384:512], tail], axis=0
    )


def unpack(w):
    tail = jnp.concatenate([w[256:288, 0:64], w[256:288, 64:128]], axis=0)
    return jnp.concatenate(
        [w[0:64], w[64:128], w[128:192], w[192:256], tail], axis=1
    )


def dot(a, b, ca, cb):
    return lax.dot_general(
        a, b, (((ca,), (cb,)), ((), ())), preferred_element_type=jnp.float32
    )


def dot_hi(a, b, ca, cb):
    return lax.dot_general(
        a, b, (((ca,), (cb,)), ((), ())),
        precision=lax.Precision.HIGHEST, preferred_element_type=jnp.float32,
    )


def gram(a, b):
    return dot_hi(a, b, 1, 1)


def combine(coef, block):
    return dot_hi(coef, block, 0, 0)


def solve(matrix, rhs):
    i = lax.broadcasted_iota(jnp.int32, (Q, Q), 0)
    j = lax.broadcasted_iota(jnp.int32, (Q, Q), 1)
    sym = jnp.where(i >= j, matrix, matrix.T)
    work = jnp.concatenate([sym, rhs], axis=1)
    line = lax.broadcasted_iota(jnp.int32, (Q, 2 * Q), 0)
    n = 8
    for k in range(0, Q, n):
        col = [jnp.broadcast_to(work[:, k + a : k + a + 1], (Q, 2 * Q)) for a in range(n)]
        row = [work[k + a : k + a + 1, :] for a in range(n)]
        piv = [[col[b][k + a : k + a + 1, :] for b in range(n)] for a in range(n)]
        for a in range(n):
            inv = 1.0 / piv[a][a]
            row[a] = row[a] * inv
            for b in range(a + 1, n):
                piv[a][b] = piv[a][b] * inv
            for other in range(n):
                if other != a:
                    f = piv[other][a]
                    row[other] = row[other] - f * row[a]
                    for b in range(a + 1, n):
                        piv[other][b] = piv[other][b] - f * piv[a][b]
        new = work
        for a in range(n):
            new = new - col[a] * row[a]
        for a in range(n):
            new = jnp.where(line == k + a, row[a], new)
        work = new
    return work[:, Q:]


def fold(g):
    return jnp.concatenate([g[0:32], g[32:64]], axis=1)


def unfold(g):
    return jnp.concatenate([g[:, 0:Q], g[:, Q:]], axis=0)


def kernel(
    rows_ref, cols_ref, counts_ref, tiles_ref, diag_ref, probes_ref,
    sol_ref, res_ref,
    blocks, diag, rp_a, rp_b, cp_a, cp_b, ps, xb, qb, r1, sb, r2, pz, zq, zin, zr2, gone,
    kept, seg_r, seg_c, prev_r, prev_c, last_r, last_c,
    ar_a, ar_ar, ar_b, ar_br, ar_c, ar_cr, ar_d, ar_dr,
    send_sem, recv_sem, tile_sem, diag_sem,
):
    z = lax.axis_index("row")
    c = lax.axis_index("col")
    y, x, k = c // 8, (c // 2) % 4, c % 2

    def at(dz=0, dy=0, dx=0, flip=False):
        kk = 1 - k if flip else k
        return (
            lax.rem(z + dz + 8, 8),
            (lax.rem(y + dy + 4, 4) * 4 + lax.rem(x + dx + 4, 4)) * 2 + kk,
        )

    def wrap(v, n):
        return lax.rem(v + 2 * n, n)

    plane_of = {0: lambda d: at(dx=d), 1: lambda d: at(dy=d)}
    rps, cps = (rp_a, rp_b), (cp_a, cp_b)
    arrivals = [0]
    sent = [0, 0]
    turn = [0]

    def group():
        arrivals[0] += 1
        return arrivals[0] - 1

    def send(src, dst, device, g):
        pltpu.make_async_remote_copy(
            src_ref=src, dst_ref=dst, send_sem=send_sem.at[turn[0]], recv_sem=recv_sem.at[g],
            device_id=device, device_id_type=MESH,
        ).start()
        width = 1 if src.dtype == jnp.bfloat16 else 2
        sent[turn[0]] += width * math.prod(src.shape) // 128

    def take(g, ref):
        pltpu.make_async_remote_copy(
            src_ref=ref, dst_ref=ref, send_sem=send_sem.at[0], recv_sem=recv_sem.at[g],
            device_id=at(flip=True), device_id_type=MESH,
        ).wait_recv()

    def drain(p):
        ref = gone.at[pl.ds(0, sent[p])]
        pltpu.make_async_remote_copy(
            src_ref=ref, dst_ref=ref, send_sem=send_sem.at[p], recv_sem=recv_sem.at[0],
            device_id=at(flip=True), device_id_type=MESH,
        ).wait_send()

    tile_copies = [
        pltpu.make_async_copy(tiles_ref.at[0, 0, s], blocks.at[s], tile_sem.at[0])
        for s in range(SLOTS)
    ]
    diag_copy = pltpu.make_async_copy(diag_ref.at[0], diag, diag_sem.at[0])

    peers = [at(dx=d) for d in STEPS] + [at(dy=d) for d in STEPS]
    peers += [at(dz=d) for d in range(1, 8)] + [at(flip=True)]
    barrier = pltpu.get_barrier_semaphore()
    for peer in peers:
        pl.semaphore_signal(barrier, inc=1, device_id=peer, device_id_type=MESH)
    pl.semaphore_wait(barrier, len(peers))

    def half(h):
        return pl.ds(h * HALF, HALF)

    def gather_begin(p, value):
        rps[p][k, y, x] = value
        cps[p][z] = value
        first = [[group() for _ in STEPS] for _ in range(2)]
        second = [[group() for _ in STEPS] for _ in range(2)]
        far, rest, across = [group(), group()], group(), group()
        own = cps[p].at[z]
        for d, g in ((2, far[0]), (-2, far[1])):
            send(own, own, at(dz=d), g)
        for i, d in enumerate(STEPS):
            for h in range(2):
                own = rps[p].at[k, y, x, half(h)]
                send(own, own, plane_of[h](d), first[h][i])
        own = cps[p].at[z]
        for d in (1, -1):
            send(own, own, at(dz=d), rest)
        for j, e in enumerate(STEPS):
            for h in range(2):
                own = rps[p].at[k, y, x, half(h)]
                send(own, own, plane_of[1 - h](e), second[h][j])
        return first, second, far, rest, across

    def gather_forward(p, state):
        first, second, far, rest, across = state
        for i, d in enumerate(STEPS):
            for h in range(2):
                ty, tx = (y, wrap(x - d, 4)) if h == 0 else (wrap(y - d, 4), x)
                got = rps[p].at[k, ty, tx, half(h)]
                take(first[h][i], got)
                for j, e in enumerate(STEPS):
                    send(got, got, plane_of[1 - h](e), second[h][j])
        for i, d in enumerate((2, -2)):
            got = cps[p].at[wrap(z - d, 8)]
            take(far[i], got)
            send(got, got, at(dz=d // 2), rest)
            got = cps[p].at[wrap(z - d, 8), half(i)]
            send(got, got, at(dz=d), rest)
        for h in range(2):
            line = rps[p].at[k, y, :, half(h)] if h == 0 else rps[p].at[k, :, x, half(h)]
            send(line, line, at(flip=True), across)

    def gather_across(p, state):
        first, second, far, rest, across = state
        for j, e in enumerate(STEPS):
            for h in range(2):
                line = (
                    rps[p].at[k, wrap(y - e, 4), :, half(h)]
                    if h == 0
                    else rps[p].at[k, :, wrap(x - e, 4), half(h)]
                )
                take(second[h][j], line)
                send(line, line, at(flip=True), across)

    def gather_end_z(p, state):
        take(state[3], cps[p].at[pl.ds(0, 5)])

    def gather_end_plane(p, state):
        take(state[4], rps[p].at[1 - k])

    def forward_products(p):
        def step(s, carry):
            far = unpack(cps[p][cols_ref[0, 0, s]])
            seg_r[s] = pack(dot(far, blocks[s], 1, 1)) + seg_r[prev_r[s]]
            return carry

        lax.fori_loop(0, SLOTS, step, 0, unroll=UNROLL)

    def mirror_products(p, low, high, cross):
        count = counts_ref[0, 0]

        def step(s, cross):
            t = rows_ref[0, 0, s]
            near = unpack(rps[p][lax.rem(t, 2), t // 8, lax.rem(t // 2, 4)])
            product = dot(near, blocks[s], 1, 0)
            seg_c[s] = pack(product) + seg_c[prev_c[s]]
            if p == 0:
                kept[s] = product.astype(jnp.bfloat16)
                return cross
            far = unpack(cps[p][cols_ref[0, 0, s]])
            held = jnp.where(s < count, 1.0, 0.0)
            return cross + held * dot(far, product.astype(jnp.bfloat16), 1, 1)

        return lax.fori_loop(low, high, step, cross, unroll=UNROLL)

    def late_cross(p, cross):
        count = counts_ref[0, 0]

        def step(s, cross):
            far = unpack(cps[p][cols_ref[0, 0, s]])
            held = jnp.where(s < count, 1.0, 0.0)
            return cross + held * dot(far, kept[s], 1, 1)

        return lax.fori_loop(0, SLOTS, step, cross, unroll=UNROLL)

    def plane_begin(p):
        def fill(kk):
            @pl.loop(0, 16)
            def _(t):
                ps[p, kk, t // 4, lax.rem(t, 4)] = seg_r[last_r[2 * t + kk]].astype(jnp.bfloat16)

        fill(1 - k)
        across = {}
        for d in ORDER:
            for h in range(2):
                across[h, d] = group()
                if h == 0:
                    t = wrap(x + d, 4)
                    src, dst = ps.at[p, 1 - k, :, t, half(h)], xb.at[p, :, t, half(h)]
                else:
                    t = wrap(y + d, 4)
                    src, dst = ps.at[p, 1 - k, t, :, half(h)], xb.at[p, t, :, half(h)]
                send(src, dst, at(flip=True), across[h, d])
        fill(k)
        return across

    def plane_stage(p, across, d):
        out = []
        for h in range(2):
            if h == 0:
                t, mine = wrap(x + d, 4), y
                take(across[h, d], xb.at[p, :, t, half(h)])
                total = ps[p, k, :, t, half(h)].astype(jnp.float32) + xb[p, :, t, half(h)].astype(jnp.float32)
            else:
                t, mine = wrap(y + d, 4), x
                take(across[h, d], xb.at[p, t, :, half(h)])
                total = ps[p, k, t, :, half(h)].astype(jnp.float32) + xb[p, t, :, half(h)].astype(jnp.float32)
            qb[p, h, d] = total.astype(jnp.bfloat16)
            g = group()
            for e in (2, 1, 3):
                send(qb.at[p, h, d, wrap(mine + e, 4)], r1.at[p, h, d, e - 1], plane_of[1 - h](e), g)
            out.append(g)
        return out

    def plane_stage2(p, mid, hooks):
        last = group()
        own = []
        for d in ORDER:
            for h in range(2):
                take(mid[d][h], r1.at[p, h, d])
                total = qb[p, h, d, y if h == 0 else x].astype(jnp.float32)
                for e in range(3):
                    total = total + r1[p, h, d, e].astype(jnp.float32)
                if d != 0:
                    sb[p, h, d] = total.astype(jnp.bfloat16)
                    send(sb.at[p, h, d], r2.at[p, h, d - 1], plane_of[h](d), last)
                else:
                    own.append(total)
            if d in hooks:
                hooks[d]()
        return last, own

    def plane_end(p, state):
        last, own = state
        take(last, r2.at[p])
        halves = []
        for h in range(2):
            total = own[h]
            for d in range(3):
                total = total + r2[p, h, d].astype(jnp.float32)
            halves.append(total)
        return jnp.concatenate(halves, axis=0)

    def z_begin(p):
        @pl.loop(0, ROWS)
        def _(t):
            pz[p, t] = seg_c[last_c[t]].astype(jnp.bfloat16)

        near, far = [group(), group()], group()
        for i, d in enumerate((1, -1)):
            send(pz.at[p, wrap(z + 3 * d, 8)], zin.at[p, i, pl.ds(0, PK)], at(dz=d), near[i])
            send(pz.at[p, wrap(z + 4, 8), half(i)], zin.at[p, i, pl.ds(PK, HALF)], at(dz=2 * d), near[i])
        for i, d in enumerate((1, -1)):
            send(pz.at[p, wrap(z + d, 8)], zr2.at[p, i], at(dz=d), far)
        return near, far

    def z_stage(p, state):
        near, far = state
        for i, d in enumerate((2, -2)):
            take(near[i], zin.at[p, i])
            total = pz[p, wrap(z + d, 8)].astype(jnp.float32) + zin[p, i, 0:PK].astype(jnp.float32)
            extra = zin[p, i, PK : PK + HALF].astype(jnp.float32)
            lo, hi = total[0:HALF], total[HALF:PK]
            if i == 0:
                lo = lo + extra
            else:
                hi = hi + extra
            zq[p, i, 0:HALF] = lo.astype(jnp.bfloat16)
            zq[p, i, HALF:PK] = hi.astype(jnp.bfloat16)
            send(zq.at[p, i], zr2.at[p, 2 + i], at(dz=d), far)

    def z_end(p, state):
        take(state[1], zr2.at[p])
        total = pz[p, z].astype(jnp.float32)
        for i in range(4):
            total = total + zr2[p, i].astype(jnp.float32)
        return total

    groups = (
        [at(flip=True)],
        [at(dx=d) for d in STEPS],
        [at(dy=d) for d in STEPS],
        [at(dz=d) for d in range(1, 8)],
    )
    bases = (0, 1, 4, 7)

    def reduce_steps(buf, rbuf, value):
        buf[0] = value
        for stage in range(4):
            g = group()
            for i, peer in enumerate(groups[stage]):
                send(buf.at[stage], rbuf.at[bases[stage] + i], peer, g)
            yield None
            total = buf[stage]
            n = len(groups[stage])
            take(g, rbuf.at[pl.ds(bases[stage], n)])
            for i in range(n):
                total = total + rbuf[bases[stage] + i]
            if stage < 3:
                buf[stage + 1] = total
        yield total

    def own_product(v):
        hi = v.astype(jnp.bfloat16)
        lo = (v - hi.astype(jnp.float32)).astype(jnp.bfloat16)
        d = diag[...]
        return dot(hi, d, 1, 1) + dot(lo, d, 1, 1)

    probes = probes_ref[0]
    state = gather_begin(0, pack(probes).astype(jnp.bfloat16))
    diag_copy.start()
    for copy in tile_copies[:8]:
        copy.start()

    count = counts_ref[0, 0]
    for s in range(SLOTS):
        pr = jnp.int32(SLOTS)
        pc = jnp.int32(SLOTS)
        for u in range(s):
            pr = jnp.where(rows_ref[0, 0, u] == rows_ref[0, 0, s], u, pr)
            pc = jnp.where(cols_ref[0, 0, u] == cols_ref[0, 0, s], u, pc)
        prev_r[s] = pr
        prev_c[s] = pc

    @pl.loop(0, PLANE)
    def _(t):
        at_slot = jnp.int32(SLOTS)
        for s in range(SLOTS):
            at_slot = jnp.where((rows_ref[0, 0, s] == t) & (s < count), s, at_slot)
        last_r[t] = at_slot

    @pl.loop(0, ROWS)
    def _(t):
        at_slot = jnp.int32(SLOTS)
        for s in range(SLOTS):
            at_slot = jnp.where((cols_ref[0, 0, s] == t) & (s < count), s, at_slot)
        last_c[t] = at_slot

    seg_r[SLOTS] = jnp.zeros((PK, 128), jnp.float32)
    seg_c[SLOTS] = jnp.zeros((PK, 128), jnp.float32)

    g00 = gram(probes, probes)
    diag_copy.wait()
    trace = jnp.zeros((1, 1), jnp.float32)
    for j in range(5):
        n = 128 if j < 4 else 64
        d = diag[pl.ds(128 * j, n), pl.ds(128 * j, n)].astype(jnp.float32)
        on = lax.broadcasted_iota(jnp.int32, (n, n), 0) == lax.broadcasted_iota(jnp.int32, (n, n), 1)
        trace = trace + jnp.sum(jnp.where(on, d, 0.0), keepdims=True)
    red_a = reduce_steps(
        ar_a, ar_ar, jnp.concatenate([fold(g00), jnp.broadcast_to(trace, (8, 128))], axis=0)
    )
    next(red_a)
    gather_forward(0, state)
    for copy in tile_copies[8:]:
        copy.start()
    next(red_a)
    own = own_product(probes)
    gather_across(0, state)
    next(red_a)
    gather_end_z(0, state)
    pltpu.make_async_copy(tiles_ref.at[0, 0], blocks, tile_sem.at[0]).wait()
    forward_products(0)
    across = plane_begin(0)
    next(red_a)
    gather_end_plane(0, state)
    mid = {}
    cross = mirror_products(0, 0, 8, jnp.zeros((Q, Q), jnp.float32))
    mid[2] = plane_stage(0, across, 2)
    cross = mirror_products(0, 8, 12, cross)
    mid[1] = plane_stage(0, across, 1)
    cross = mirror_products(0, 12, 16, cross)
    zs = z_begin(0)
    mid[3] = plane_stage(0, across, 3)
    mid[0] = plane_stage(0, across, 0)
    cross = late_cross(0, cross)
    cross = cross + cross.T
    red_b = reduce_steps(ar_b, ar_br, fold(gram(probes, own) + cross))
    next(red_b)
    total = next(red_a)
    rr0 = unfold(total[0:32])
    shift = total[32:33, 0:1] * (1.0 / (NT * B))
    eye = (
        lax.broadcasted_iota(jnp.int32, (Q, Q), 0) == lax.broadcasted_iota(jnp.int32, (Q, Q), 1)
    ).astype(jnp.float32)
    offset = pack(own - shift * probes)
    next(red_b)
    z_stage(0, zs)
    inverse = []

    def after_sends():
        next(red_b)
        inverse.append(solve(rr0, eye))

    last = plane_stage2(0, mid, {2: lambda: next(red_b), 3: after_sends})
    rr0_inv = inverse[0]
    packed = offset + z_end(0, zs)
    packed = packed + plane_end(0, last)

    turn[0] = 1
    state = gather_begin(1, packed.astype(jnp.bfloat16))
    basis = unpack(packed)
    image = basis + shift * probes
    red_c = reduce_steps(ar_c, ar_cr, fold(gram(basis, basis)))
    next(red_c)
    own = own_product(basis)
    gather_forward(1, state)
    next(red_c)
    pq0 = unfold(next(red_b))
    alpha = solve(pq0, rr0)
    drain(0)
    gather_across(1, state)
    next(red_c)
    gather_end_z(1, state)
    forward_products(1)
    across = plane_begin(1)
    next(red_c)
    gather_end_plane(1, state)
    mid = {}
    cross = mirror_products(1, 0, 8, jnp.zeros((Q, Q), jnp.float32))
    mid[2] = plane_stage(1, across, 2)
    cross = mirror_products(1, 8, 12, cross)
    mid[1] = plane_stage(1, across, 1)
    cross = mirror_products(1, 12, 16, cross)
    cross = cross + cross.T
    zs = z_begin(1)
    red_d = reduce_steps(ar_d, ar_dr, fold(gram(basis, own) + cross))
    next(red_d)
    mid[3] = plane_stage(1, across, 3)
    mid[0] = plane_stage(1, across, 0)
    next(red_d)
    g11 = unfold(next(red_c))
    g01 = pq0 - shift * rr0
    m0 = eye - shift * alpha
    m1 = -alpha
    rr1 = (
        dot_hi(m0, dot_hi(rr0, m0, 1, 0) + dot_hi(g01, m1, 1, 0), 0, 0)
        + dot_hi(m1, dot_hi(g01, m0, 0, 0) + dot_hi(g11, m1, 1, 0), 0, 0)
    )
    beta = dot_hi(rr0_inv, rr1, 1, 0)
    n0 = m0 + beta
    residual = combine(m0, probes) + combine(m1, basis)
    next(red_d)
    z_stage(1, zs)
    next(red_d)
    direction = residual + combine(beta, probes)
    xsol = combine(alpha, probes)
    partial = combine(n0, image)
    g02 = g11 + shift * g01
    known = dot_hi(n0, dot_hi(pq0, n0, 1, 0) + dot_hi(g02, m1, 1, 0), 0, 0) + dot_hi(
        m1, dot_hi(g02, n0, 0, 0), 0, 0
    )
    found = []

    def finish():
        g12 = unfold(next(red_d))
        found.append(solve(known + dot_hi(m1, dot_hi(g12, m1, 1, 0), 0, 0), rr1))

    last = plane_stage2(1, mid, {3: finish})
    drain(1)
    gamma = found[0]
    deep = z_end(1, zs)
    deep = deep + plane_end(1, last)
    image2 = partial + combine(m1, own + unpack(deep))
    sol_ref[...] = xsol + combine(gamma, direction)
    res_ref[...] = residual - combine(gamma, image2)


def close(sol_ref, res_ref, sol_out, res_out):
    sol_out[0] = sol_ref[...]
    res_out[0] = res_ref[...]


def body(tiles, diag_tiles, probes, rows_list, cols_list, counts):
    smem = pl.BlockSpec(memory_space=pltpu.SMEM)
    vmem = pl.BlockSpec(memory_space=pltpu.VMEM)
    hbm = pl.BlockSpec(memory_space=pl.ANY)
    bf, f32, i32 = jnp.bfloat16, jnp.float32, jnp.int32
    wide = jax.ShapeDtypeStruct((Q, B), f32)
    parts = pl.pallas_call(
        kernel,
        out_shape=(wide, wide),
        in_specs=[smem, smem, smem, hbm, hbm, vmem],
        out_specs=(vmem, vmem),
        scratch_shapes=[
            pltpu.VMEM((SLOTS, B, B), bf),
            pltpu.VMEM((B, B), bf),
            pltpu.VMEM((2, 4, 4, PK, 128), bf),
            pltpu.VMEM((2, 4, 4, PK, 128), bf),
            pltpu.VMEM((ROWS, PK, 128), bf),
            pltpu.VMEM((ROWS, PK, 128), bf),
            pltpu.VMEM((2, 2, 4, 4, PK, 128), bf),
            pltpu.VMEM((2, 4, 4, PK, 128), bf),
            pltpu.VMEM((2, 2, 4, 4, HALF, 128), bf),
            pltpu.VMEM((2, 2, 4, 3, HALF, 128), bf),
            pltpu.VMEM((2, 2, 4, HALF, 128), bf),
            pltpu.VMEM((2, 2, 3, HALF, 128), bf),
            pltpu.VMEM((2, ROWS, PK, 128), bf),
            pltpu.VMEM((2, 2, PK, 128), bf),
            pltpu.VMEM((2, 2, PK + HALF, 128), bf),
            pltpu.VMEM((2, 4, PK, 128), bf),
            pltpu.VMEM((SENT, 128), bf),
            pltpu.VMEM((SLOTS, Q, B), bf),
            pltpu.VMEM((SLOTS + 1, PK, 128), f32),
            pltpu.VMEM((SLOTS + 1, PK, 128), f32),
            pltpu.SMEM((SLOTS,), i32),
            pltpu.SMEM((SLOTS,), i32),
            pltpu.SMEM((PLANE,), i32),
            pltpu.SMEM((ROWS,), i32),
            pltpu.VMEM((4, 40, 128), f32),
            pltpu.VMEM((14, 40, 128), f32),
            pltpu.VMEM((4, 32, 128), f32),
            pltpu.VMEM((14, 32, 128), f32),
            pltpu.VMEM((4, 32, 128), f32),
            pltpu.VMEM((14, 32, 128), f32),
            pltpu.VMEM((4, 32, 128), f32),
            pltpu.VMEM((14, 32, 128), f32),
            pltpu.SemaphoreType.DMA((2,)),
            pltpu.SemaphoreType.DMA((N_ARRIVALS,)),
            pltpu.SemaphoreType.DMA((1,)),
            pltpu.SemaphoreType.DMA((1,)),
        ],
        compiler_params=pltpu.CompilerParams(
            collective_id=0, has_side_effects=True, vmem_limit_bytes=56 << 20
        ),
        name="block_cg",
    )(rows_list, cols_list, counts, tiles, diag_tiles, probes)
    return pl.pallas_call(
        close,
        out_shape=(jax.ShapeDtypeStruct((1, Q, B), f32),) * 2,
        in_specs=[vmem] * 2,
        out_specs=(vmem, vmem),
        name="close",
    )(*parts)


def solution(mesh):
    placed = (
        P("row", "col", None, None, None),
        P(("row", "col"), None, None),
        P(("row", "col"), None, None),
        P("row", "col", None),
        P("row", "col", None),
        P("row", "col"),
    )
    return jax.shard_map(
        body,
        mesh=mesh,
        in_specs=placed,
        out_specs=(P(("row", "col"), None, None), P(("row", "col"), None, None)),
        check_vma=False,
    )
```

```python
import math

import jax
import jax.numpy as jnp
from jax import lax
from jax.experimental import pallas as pl
from jax.experimental.pallas import tpu as pltpu
from jax.sharding import PartitionSpec as P

MESH = pl.DeviceIdType.MESH
B, Q, SLOTS, ROWS, PLANE = 576, 64, 16, 8, 32
PK, HALF = 288, 144
STEPS = (1, 3, 2)
ORDER = (2, 1, 3, 0)
N_ARRIVALS = 92
SENT = 26000
NT = 256
UNROLL = 4


def pack(v):
    tail = jnp.concatenate([v[0:32, 512:576], v[32:64, 512:576]], axis=1)
    return jnp.concatenate(
        [v[:, 0:128], v[:, 128:256], v[:, 256:384], v[:, 384:512], tail], axis=0
    )


def unpack(w):
    tail = jnp.concatenate([w[256:288, 0:64], w[256:288, 64:128]], axis=0)
    return jnp.concatenate(
        [w[0:64], w[64:128], w[128:192], w[192:256], tail], axis=1
    )


def dot(a, b, ca, cb):
    return lax.dot_general(
        a, b, (((ca,), (cb,)), ((), ())), preferred_element_type=jnp.float32
    )


def dot_hi(a, b, ca, cb):
    return lax.dot_general(
        a, b, (((ca,), (cb,)), ((), ())),
        precision=lax.Precision.HIGHEST, preferred_element_type=jnp.float32,
    )


def gram(a, b):
    return dot_hi(a, b, 1, 1)


def combine(coef, block):
    return dot_hi(coef, block, 0, 0)


def solve(matrix, rhs):
    i = lax.broadcasted_iota(jnp.int32, (Q, Q), 0)
    j = lax.broadcasted_iota(jnp.int32, (Q, Q), 1)
    sym = jnp.where(i >= j, matrix, matrix.T)
    work = jnp.concatenate([sym, rhs], axis=1)
    line = lax.broadcasted_iota(jnp.int32, (Q, 2 * Q), 0)
    n = 8
    for k in range(0, Q, n):
        col = [jnp.broadcast_to(work[:, k + a : k + a + 1], (Q, 2 * Q)) for a in range(n)]
        row = [work[k + a : k + a + 1, :] for a in range(n)]
        piv = [[col[b][k + a : k + a + 1, :] for b in range(n)] for a in range(n)]
        for a in range(n):
            inv = 1.0 / piv[a][a]
            row[a] = row[a] * inv
            for b in range(a + 1, n):
                piv[a][b] = piv[a][b] * inv
            for other in range(n):
                if other != a:
                    f = piv[other][a]
                    row[other] = row[other] - f * row[a]
                    for b in range(a + 1, n):
                        piv[other][b] = piv[other][b] - f * piv[a][b]
        new = work
        for a in range(n):
            new = new - col[a] * row[a]
        for a in range(n):
            new = jnp.where(line == k + a, row[a], new)
        work = new
    return work[:, Q:]


def fold(g):
    return jnp.concatenate([g[0:32], g[32:64]], axis=1)


def unfold(g):
    return jnp.concatenate([g[:, 0:Q], g[:, Q:]], axis=0)


def kernel(
    rows_ref, cols_ref, counts_ref, tiles_ref, diag_ref, probes_ref,
    sol_ref, res_ref,
    blocks, diag, rp_a, rp_b, cp_a, cp_b, ps, xb, qb, r1, sb, r2, pz, zq, zin, zr2, gone,
    kept, seg_r, seg_c, prev_r, prev_c, last_r, last_c,
    ar_a, ar_ar, ar_b, ar_br, ar_c, ar_cr, ar_d, ar_dr,
    send_sem, recv_sem, tile_sem, diag_sem,
):
    z = lax.axis_index("row")
    c = lax.axis_index("col")
    y, x, k = c // 8, (c // 2) % 4, c % 2

    def at(dz=0, dy=0, dx=0, flip=False):
        kk = 1 - k if flip else k
        return (
            lax.rem(z + dz + 8, 8),
            (lax.rem(y + dy + 4, 4) * 4 + lax.rem(x + dx + 4, 4)) * 2 + kk,
        )

    def wrap(v, n):
        return lax.rem(v + 2 * n, n)

    plane_of = {0: lambda d: at(dx=d), 1: lambda d: at(dy=d)}
    rps, cps = (rp_a, rp_b), (cp_a, cp_b)
    arrivals = [0]
    sent = [0, 0]
    turn = [0]

    def group():
        arrivals[0] += 1
        return arrivals[0] - 1

    def send(src, dst, device, g):
        pltpu.make_async_remote_copy(
            src_ref=src, dst_ref=dst, send_sem=send_sem.at[turn[0]], recv_sem=recv_sem.at[g],
            device_id=device, device_id_type=MESH,
        ).start()
        width = 1 if src.dtype == jnp.bfloat16 else 2
        sent[turn[0]] += width * math.prod(src.shape) // 128

    def take(g, ref):
        pltpu.make_async_remote_copy(
            src_ref=ref, dst_ref=ref, send_sem=send_sem.at[0], recv_sem=recv_sem.at[g],
            device_id=at(flip=True), device_id_type=MESH,
        ).wait_recv()

    def drain(p):
        ref = gone.at[pl.ds(0, sent[p])]
        pltpu.make_async_remote_copy(
            src_ref=ref, dst_ref=ref, send_sem=send_sem.at[p], recv_sem=recv_sem.at[0],
            device_id=at(flip=True), device_id_type=MESH,
        ).wait_send()

    tile_copies = [
        pltpu.make_async_copy(tiles_ref.at[0, 0, s], blocks.at[s], tile_sem.at[0])
        for s in range(SLOTS)
    ]
    diag_copy = pltpu.make_async_copy(diag_ref.at[0], diag, diag_sem.at[0])

    peers = [at(dx=d) for d in STEPS] + [at(dy=d) for d in STEPS]
    peers += [at(dz=d) for d in range(1, 8)] + [at(flip=True)]
    barrier = pltpu.get_barrier_semaphore()
    for peer in peers:
        pl.semaphore_signal(barrier, inc=1, device_id=peer, device_id_type=MESH)
    pl.semaphore_wait(barrier, len(peers))

    def half(h):
        return pl.ds(h * HALF, HALF)

    def gather_begin(p, value):
        rps[p][k, y, x] = value
        cps[p][z] = value
        first = [[group() for _ in STEPS] for _ in range(2)]
        second = [[group() for _ in STEPS] for _ in range(2)]
        far, rest, across = [group(), group()], group(), group()
        own = cps[p].at[z]
        for d, g in ((2, far[0]), (-2, far[1])):
            send(own, own, at(dz=d), g)
        for i, d in enumerate(STEPS):
            for h in range(2):
                own = rps[p].at[k, y, x, half(h)]
                send(own, own, plane_of[h](d), first[h][i])
        own = cps[p].at[z]
        for d in (1, -1):
            send(own, own, at(dz=d), rest)
        for j, e in enumerate(STEPS):
            for h in range(2):
                own = rps[p].at[k, y, x, half(h)]
                send(own, own, plane_of[1 - h](e), second[h][j])
        return first, second, far, rest, across

    def gather_forward(p, state):
        first, second, far, rest, across = state
        for i, d in enumerate(STEPS):
            for h in range(2):
                ty, tx = (y, wrap(x - d, 4)) if h == 0 else (wrap(y - d, 4), x)
                got = rps[p].at[k, ty, tx, half(h)]
                take(first[h][i], got)
                for j, e in enumerate(STEPS):
                    send(got, got, plane_of[1 - h](e), second[h][j])
        for i, d in enumerate((2, -2)):
            got = cps[p].at[wrap(z - d, 8)]
            take(far[i], got)
            send(got, got, at(dz=d // 2), rest)
            got = cps[p].at[wrap(z - d, 8), half(i)]
            send(got, got, at(dz=d), rest)
        for h in range(2):
            line = rps[p].at[k, y, :, half(h)] if h == 0 else rps[p].at[k, :, x, half(h)]
            send(line, line, at(flip=True), across)

    def gather_across(p, state):
        first, second, far, rest, across = state
        for j, e in enumerate(STEPS):
            for h in range(2):
                line = (
                    rps[p].at[k, wrap(y - e, 4), :, half(h)]
                    if h == 0
                    else rps[p].at[k, :, wrap(x - e, 4), half(h)]
                )
                take(second[h][j], line)
                send(line, line, at(flip=True), across)

    def gather_end_z(p, state):
        take(state[3], cps[p].at[pl.ds(0, 5)])

    def gather_end_plane(p, state):
        take(state[4], rps[p].at[1 - k])

    def forward_products(p):
        def step(s, carry):
            far = unpack(cps[p][cols_ref[0, 0, s]])
            seg_r[s] = pack(dot(far, blocks[s], 1, 1)) + seg_r[prev_r[s]]
            return carry

        lax.fori_loop(0, SLOTS, step, 0, unroll=UNROLL)

    def mirror_products(p, low, high, cross):
        count = counts_ref[0, 0]

        def step(s, cross):
            t = rows_ref[0, 0, s]
            near = unpack(rps[p][lax.rem(t, 2), t // 8, lax.rem(t // 2, 4)])
            product = dot(near, blocks[s], 1, 0)
            seg_c[s] = pack(product) + seg_c[prev_c[s]]
            if p == 0:
                kept[s] = product.astype(jnp.bfloat16)
                return cross
            far = unpack(cps[p][cols_ref[0, 0, s]])
            held = jnp.where(s < count, 1.0, 0.0)
            return cross + held * dot(far, product.astype(jnp.bfloat16), 1, 1)

        return lax.fori_loop(low, high, step, cross, unroll=UNROLL)

    def late_cross(p, cross):
        count = counts_ref[0, 0]

        def step(s, cross):
            far = unpack(cps[p][cols_ref[0, 0, s]])
            held = jnp.where(s < count, 1.0, 0.0)
            return cross + held * dot(far, kept[s], 1, 1)

        return lax.fori_loop(0, SLOTS, step, cross, unroll=UNROLL)

    def plane_begin(p):
        def fill(kk):
            @pl.loop(0, 16, unroll=4)
            def _(t):
                ps[p, kk, t // 4, lax.rem(t, 4)] = seg_r[last_r[2 * t + kk]].astype(jnp.bfloat16)

        fill(1 - k)
        across = {}
        for d in ORDER:
            for h in range(2):
                across[h, d] = group()
                if h == 0:
                    t = wrap(x + d, 4)
                    src, dst = ps.at[p, 1 - k, :, t, half(h)], xb.at[p, :, t, half(h)]
                else:
                    t = wrap(y + d, 4)
                    src, dst = ps.at[p, 1 - k, t, :, half(h)], xb.at[p, t, :, half(h)]
                send(src, dst, at(flip=True), across[h, d])
        fill(k)
        return across

    def plane_stage(p, across, d):
        out = []
        for h in range(2):
            if h == 0:
                t, mine = wrap(x + d, 4), y
                take(across[h, d], xb.at[p, :, t, half(h)])
                total = ps[p, k, :, t, half(h)].astype(jnp.float32) + xb[p, :, t, half(h)].astype(jnp.float32)
            else:
                t, mine = wrap(y + d, 4), x
                take(across[h, d], xb.at[p, t, :, half(h)])
                total = ps[p, k, t, :, half(h)].astype(jnp.float32) + xb[p, t, :, half(h)].astype(jnp.float32)
            qb[p, h, d] = total.astype(jnp.bfloat16)
            g = group()
            for e in (2, 1, 3):
                send(qb.at[p, h, d, wrap(mine + e, 4)], r1.at[p, h, d, e - 1], plane_of[1 - h](e), g)
            out.append(g)
        return out

    def plane_stage2(p, mid, hooks):
        last = group()
        own = []
        for d in ORDER:
            for h in range(2):
                take(mid[d][h], r1.at[p, h, d])
                total = qb[p, h, d, y if h == 0 else x].astype(jnp.float32)
                for e in range(3):
                    total = total + r1[p, h, d, e].astype(jnp.float32)
                if d != 0:
                    sb[p, h, d] = total.astype(jnp.bfloat16)
                    send(sb.at[p, h, d], r2.at[p, h, d - 1], plane_of[h](d), last)
                else:
                    own.append(total)
            if d in hooks:
                hooks[d]()
        return last, own

    def plane_end(p, state):
        last, own = state
        take(last, r2.at[p])
        halves = []
        for h in range(2):
            total = own[h]
            for d in range(3):
                total = total + r2[p, h, d].astype(jnp.float32)
            halves.append(total)
        return jnp.concatenate(halves, axis=0)

    def z_begin(p):
        @pl.loop(0, ROWS, unroll=4)
        def _(t):
            pz[p, t] = seg_c[last_c[t]].astype(jnp.bfloat16)

        near, far = [group(), group()], group()
        for i, d in enumerate((1, -1)):
            send(pz.at[p, wrap(z + 3 * d, 8)], zin.at[p, i, pl.ds(0, PK)], at(dz=d), near[i])
            send(pz.at[p, wrap(z + 4, 8), half(i)], zin.at[p, i, pl.ds(PK, HALF)], at(dz=2 * d), near[i])
        for i, d in enumerate((1, -1)):
            send(pz.at[p, wrap(z + d, 8)], zr2.at[p, i], at(dz=d), far)
        return near, far

    def z_stage(p, state):
        near, far = state
        for i, d in enumerate((2, -2)):
            take(near[i], zin.at[p, i])
            total = pz[p, wrap(z + d, 8)].astype(jnp.float32) + zin[p, i, 0:PK].astype(jnp.float32)
            extra = zin[p, i, PK : PK + HALF].astype(jnp.float32)
            lo, hi = total[0:HALF], total[HALF:PK]
            if i == 0:
                lo = lo + extra
            else:
                hi = hi + extra
            zq[p, i, 0:HALF] = lo.astype(jnp.bfloat16)
            zq[p, i, HALF:PK] = hi.astype(jnp.bfloat16)
            send(zq.at[p, i], zr2.at[p, 2 + i], at(dz=d), far)

    def z_end(p, state):
        take(state[1], zr2.at[p])
        total = pz[p, z].astype(jnp.float32)
        for i in range(4):
            total = total + zr2[p, i].astype(jnp.float32)
        return total

    groups = (
        [at(flip=True)],
        [at(dx=d) for d in STEPS],
        [at(dy=d) for d in STEPS],
        [at(dz=d) for d in range(1, 8)],
    )
    bases = (0, 1, 4, 7)

    def reduce_steps(buf, rbuf, value):
        buf[0] = value
        for stage in range(4):
            g = group()
            for i, peer in enumerate(groups[stage]):
                send(buf.at[stage], rbuf.at[bases[stage] + i], peer, g)
            yield None
            total = buf[stage]
            n = len(groups[stage])
            take(g, rbuf.at[pl.ds(bases[stage], n)])
            for i in range(n):
                total = total + rbuf[bases[stage] + i]
            if stage < 3:
                buf[stage + 1] = total
        yield total

    def own_product(v):
        hi = v.astype(jnp.bfloat16)
        lo = (v - hi.astype(jnp.float32)).astype(jnp.bfloat16)
        d = diag[...]
        return dot(hi, d, 1, 1) + dot(lo, d, 1, 1)

    probes = probes_ref[0]
    state = gather_begin(0, pack(probes).astype(jnp.bfloat16))
    diag_copy.start()
    for copy in tile_copies[:8]:
        copy.start()

    count = counts_ref[0, 0]
    for s in range(SLOTS):
        pr = jnp.int32(SLOTS)
        pc = jnp.int32(SLOTS)
        for u in range(s):
            pr = jnp.where(rows_ref[0, 0, u] == rows_ref[0, 0, s], u, pr)
            pc = jnp.where(cols_ref[0, 0, u] == cols_ref[0, 0, s], u, pc)
        prev_r[s] = pr
        prev_c[s] = pc

    @pl.loop(0, PLANE)
    def _(t):
        at_slot = jnp.int32(SLOTS)
        for s in range(SLOTS):
            at_slot = jnp.where((rows_ref[0, 0, s] == t) & (s < count), s, at_slot)
        last_r[t] = at_slot

    @pl.loop(0, ROWS)
    def _(t):
        at_slot = jnp.int32(SLOTS)
        for s in range(SLOTS):
            at_slot = jnp.where((cols_ref[0, 0, s] == t) & (s < count), s, at_slot)
        last_c[t] = at_slot

    seg_r[SLOTS] = jnp.zeros((PK, 128), jnp.float32)
    seg_c[SLOTS] = jnp.zeros((PK, 128), jnp.float32)

    g00 = gram(probes, probes)
    diag_copy.wait()
    trace = jnp.zeros((1, 1), jnp.float32)
    for j in range(5):
        n = 128 if j < 4 else 64
        d = diag[pl.ds(128 * j, n), pl.ds(128 * j, n)].astype(jnp.float32)
        on = lax.broadcasted_iota(jnp.int32, (n, n), 0) == lax.broadcasted_iota(jnp.int32, (n, n), 1)
        trace = trace + jnp.sum(jnp.where(on, d, 0.0), keepdims=True)
    red_a = reduce_steps(
        ar_a, ar_ar, jnp.concatenate([fold(g00), jnp.broadcast_to(trace, (8, 128))], axis=0)
    )
    next(red_a)
    gather_forward(0, state)
    for copy in tile_copies[8:]:
        copy.start()
    next(red_a)
    own = own_product(probes)
    gather_across(0, state)
    next(red_a)
    gather_end_z(0, state)
    pltpu.make_async_copy(tiles_ref.at[0, 0], blocks, tile_sem.at[0]).wait()
    forward_products(0)
    across = plane_begin(0)
    next(red_a)
    gather_end_plane(0, state)
    mid = {}
    cross = mirror_products(0, 0, 8, jnp.zeros((Q, Q), jnp.float32))
    mid[2] = plane_stage(0, across, 2)
    cross = mirror_products(0, 8, 12, cross)
    mid[1] = plane_stage(0, across, 1)
    cross = mirror_products(0, 12, 16, cross)
    zs = z_begin(0)
    mid[3] = plane_stage(0, across, 3)
    mid[0] = plane_stage(0, across, 0)
    cross = late_cross(0, cross)
    cross = cross + cross.T
    red_b = reduce_steps(ar_b, ar_br, fold(gram(probes, own) + cross))
    next(red_b)
    total = next(red_a)
    rr0 = unfold(total[0:32])
    shift = total[32:33, 0:1] * (1.0 / (NT * B))
    eye = (
        lax.broadcasted_iota(jnp.int32, (Q, Q), 0) == lax.broadcasted_iota(jnp.int32, (Q, Q), 1)
    ).astype(jnp.float32)
    offset = pack(own - shift * probes)
    next(red_b)
    z_stage(0, zs)
    last = plane_stage2(0, mid, {1: lambda: next(red_b), 3: lambda: next(red_b)})
    packed = offset + z_end(0, zs)
    packed = packed + plane_end(0, last)

    turn[0] = 1
    state = gather_begin(1, packed.astype(jnp.bfloat16))
    basis = unpack(packed)
    image = basis + shift * probes
    red_c = reduce_steps(ar_c, ar_cr, fold(gram(basis, basis)))
    next(red_c)
    rr0_inv = solve(rr0, eye)
    gather_forward(1, state)
    next(red_c)
    own = own_product(basis)
    pq0 = unfold(next(red_b))
    alpha = solve(pq0, rr0)
    drain(0)
    gather_across(1, state)
    next(red_c)
    gather_end_z(1, state)
    forward_products(1)
    across = plane_begin(1)
    next(red_c)
    gather_end_plane(1, state)
    mid = {}
    cross = mirror_products(1, 0, 8, jnp.zeros((Q, Q), jnp.float32))
    mid[2] = plane_stage(1, across, 2)
    cross = mirror_products(1, 8, 12, cross)
    mid[1] = plane_stage(1, across, 1)
    cross = mirror_products(1, 12, 16, cross)
    cross = cross + cross.T
    zs = z_begin(1)
    red_d = reduce_steps(ar_d, ar_dr, fold(gram(basis, own) + cross))
    next(red_d)
    mid[3] = plane_stage(1, across, 3)
    mid[0] = plane_stage(1, across, 0)
    next(red_d)
    g11 = unfold(next(red_c))
    g01 = pq0 - shift * rr0
    m0 = eye - shift * alpha
    m1 = -alpha
    rr1 = (
        dot_hi(m0, dot_hi(rr0, m0, 1, 0) + dot_hi(g01, m1, 1, 0), 0, 0)
        + dot_hi(m1, dot_hi(g01, m0, 0, 0) + dot_hi(g11, m1, 1, 0), 0, 0)
    )
    beta = dot_hi(rr0_inv, rr1, 1, 0)
    n0 = m0 + beta
    next(red_d)
    g02 = g11 + shift * g01
    known = dot_hi(n0, dot_hi(pq0, n0, 1, 0) + dot_hi(g02, m1, 1, 0), 0, 0) + dot_hi(
        m1, dot_hi(g02, n0, 0, 0), 0, 0
    )
    z_stage(1, zs)
    next(red_d)
    found = []

    def finish():
        residual = combine(m0, probes) + combine(m1, basis)
        direction = residual + combine(beta, probes)
        xsol = combine(alpha, probes)
        partial = combine(n0, image) + combine(m1, own)
        g12 = unfold(next(red_d))
        gamma = solve(known + dot_hi(m1, dot_hi(g12, m1, 1, 0), 0, 0), rr1)
        found.extend((residual, direction, xsol, partial, gamma))

    last = plane_stage2(1, mid, {3: finish})
    drain(1)
    residual, direction, xsol, partial, gamma = found
    deep = z_end(1, zs)
    deep = deep + plane_end(1, last)
    image2 = partial + combine(m1, unpack(deep))
    sol_ref[...] = xsol + combine(gamma, direction)
    res_ref[...] = residual - combine(gamma, image2)


def close(sol_ref, res_ref, sol_out, res_out):
    sol_out[0] = sol_ref[...]
    res_out[0] = res_ref[...]


def body(tiles, diag_tiles, probes, rows_list, cols_list, counts):
    smem = pl.BlockSpec(memory_space=pltpu.SMEM)
    vmem = pl.BlockSpec(memory_space=pltpu.VMEM)
    hbm = pl.BlockSpec(memory_space=pl.ANY)
    bf, f32, i32 = jnp.bfloat16, jnp.float32, jnp.int32
    wide = jax.ShapeDtypeStruct((Q, B), f32)
    parts = pl.pallas_call(
        kernel,
        out_shape=(wide, wide),
        in_specs=[smem, smem, smem, hbm, hbm, vmem],
        out_specs=(vmem, vmem),
        scratch_shapes=[
            pltpu.VMEM((SLOTS, B, B), bf),
            pltpu.VMEM((B, B), bf),
            pltpu.VMEM((2, 4, 4, PK, 128), bf),
            pltpu.VMEM((2, 4, 4, PK, 128), bf),
            pltpu.VMEM((ROWS, PK, 128), bf),
            pltpu.VMEM((ROWS, PK, 128), bf),
            pltpu.VMEM((2, 2, 4, 4, PK, 128), bf),
            pltpu.VMEM((2, 4, 4, PK, 128), bf),
            pltpu.VMEM((2, 2, 4, 4, HALF, 128), bf),
            pltpu.VMEM((2, 2, 4, 3, HALF, 128), bf),
            pltpu.VMEM((2, 2, 4, HALF, 128), bf),
            pltpu.VMEM((2, 2, 3, HALF, 128), bf),
            pltpu.VMEM((2, ROWS, PK, 128), bf),
            pltpu.VMEM((2, 2, PK, 128), bf),
            pltpu.VMEM((2, 2, PK + HALF, 128), bf),
            pltpu.VMEM((2, 4, PK, 128), bf),
            pltpu.VMEM((SENT, 128), bf),
            pltpu.VMEM((SLOTS, Q, B), bf),
            pltpu.VMEM((SLOTS + 1, PK, 128), f32),
            pltpu.VMEM((SLOTS + 1, PK, 128), f32),
            pltpu.SMEM((SLOTS,), i32),
            pltpu.SMEM((SLOTS,), i32),
            pltpu.SMEM((PLANE,), i32),
            pltpu.SMEM((ROWS,), i32),
            pltpu.VMEM((4, 40, 128), f32),
            pltpu.VMEM((14, 40, 128), f32),
            pltpu.VMEM((4, 32, 128), f32),
            pltpu.VMEM((14, 32, 128), f32),
            pltpu.VMEM((4, 32, 128), f32),
            pltpu.VMEM((14, 32, 128), f32),
            pltpu.VMEM((4, 32, 128), f32),
            pltpu.VMEM((14, 32, 128), f32),
            pltpu.SemaphoreType.DMA((2,)),
            pltpu.SemaphoreType.DMA((N_ARRIVALS,)),
            pltpu.SemaphoreType.DMA((1,)),
            pltpu.SemaphoreType.DMA((1,)),
        ],
        compiler_params=pltpu.CompilerParams(
            collective_id=0, has_side_effects=True, vmem_limit_bytes=56 << 20
        ),
        name="block_cg",
    )(rows_list, cols_list, counts, tiles, diag_tiles, probes)
    return pl.pallas_call(
        close,
        out_shape=(jax.ShapeDtypeStruct((1, Q, B), f32),) * 2,
        in_specs=[vmem] * 2,
        out_specs=(vmem, vmem),
        name="close",
    )(*parts)


def solution(mesh):
    placed = (
        P("row", "col", None, None, None),
        P(("row", "col"), None, None),
        P(("row", "col"), None, None),
        P("row", "col", None),
        P("row", "col", None),
        P("row", "col"),
    )
    return jax.shard_map(
        body,
        mesh=mesh,
        in_specs=placed,
        out_specs=(P(("row", "col"), None, None), P(("row", "col"), None, None)),
        check_vma=False,
    )
```

```python
import math

import jax
import jax.numpy as jnp
from jax import lax
from jax.experimental import pallas as pl
from jax.experimental.pallas import tpu as pltpu
from jax.sharding import PartitionSpec as P

MESH = pl.DeviceIdType.MESH
B, Q, SLOTS, ROWS, PLANE = 576, 64, 16, 8, 32
PK, HALF = 288, 144
STEPS = (1, 3, 2)
ORDER = (2, 1, 3, 0)
N_ARRIVALS = 92
SENT = 26000
NT = 256
UNROLL = 4


def pack(v):
    tail = jnp.concatenate([v[0:32, 512:576], v[32:64, 512:576]], axis=1)
    return jnp.concatenate(
        [v[:, 0:128], v[:, 128:256], v[:, 256:384], v[:, 384:512], tail], axis=0
    )


def unpack(w):
    tail = jnp.concatenate([w[256:288, 0:64], w[256:288, 64:128]], axis=0)
    return jnp.concatenate(
        [w[0:64], w[64:128], w[128:192], w[192:256], tail], axis=1
    )


def dot(a, b, ca, cb):
    return lax.dot_general(
        a, b, (((ca,), (cb,)), ((), ())), preferred_element_type=jnp.float32
    )


def dot_hi(a, b, ca, cb):
    return lax.dot_general(
        a, b, (((ca,), (cb,)), ((), ())),
        precision=lax.Precision.HIGHEST, preferred_element_type=jnp.float32,
    )


def gram(a, b):
    return dot_hi(a, b, 1, 1)


def combine(coef, block):
    return dot_hi(coef, block, 0, 0)


def solve(matrix, rhs):
    i = lax.broadcasted_iota(jnp.int32, (Q, Q), 0)
    j = lax.broadcasted_iota(jnp.int32, (Q, Q), 1)
    sym = jnp.where(i >= j, matrix, matrix.T)
    work = jnp.concatenate([sym, rhs], axis=1)
    line = lax.broadcasted_iota(jnp.int32, (Q, 2 * Q), 0)
    n = 8
    for k in range(0, Q, n):
        col = [jnp.broadcast_to(work[:, k + a : k + a + 1], (Q, 2 * Q)) for a in range(n)]
        row = [work[k + a : k + a + 1, :] for a in range(n)]
        piv = [[col[b][k + a : k + a + 1, :] for b in range(n)] for a in range(n)]
        for a in range(n):
            inv = 1.0 / piv[a][a]
            row[a] = row[a] * inv
            for b in range(a + 1, n):
                piv[a][b] = piv[a][b] * inv
            for other in range(n):
                if other != a:
                    f = piv[other][a]
                    row[other] = row[other] - f * row[a]
                    for b in range(a + 1, n):
                        piv[other][b] = piv[other][b] - f * piv[a][b]
        new = work
        for a in range(n):
            new = new - col[a] * row[a]
        for a in range(n):
            new = jnp.where(line == k + a, row[a], new)
        work = new
    return work[:, Q:]


def fold(g):
    return jnp.concatenate([g[0:32], g[32:64]], axis=1)


def unfold(g):
    return jnp.concatenate([g[:, 0:Q], g[:, Q:]], axis=0)


def kernel(
    rows_ref, cols_ref, counts_ref, tiles_ref, diag_ref, probes_ref,
    sol_ref, res_ref,
    blocks, diag, rp_a, rp_b, cp_a, cp_b, ps, xb, qb, r1, sb, r2, pz, zq, zin, zr2, gone,
    kept, seg_r, seg_c, prev_r, prev_c, last_r, last_c,
    ar_a, ar_ar, ar_b, ar_br, ar_c, ar_cr, ar_d, ar_dr,
    send_sem, recv_sem, tile_sem, diag_sem,
):
    z = lax.axis_index("row")
    c = lax.axis_index("col")
    y, x, k = c // 8, (c // 2) % 4, c % 2

    def at(dz=0, dy=0, dx=0, flip=False):
        kk = 1 - k if flip else k
        return (
            lax.rem(z + dz + 8, 8),
            (lax.rem(y + dy + 4, 4) * 4 + lax.rem(x + dx + 4, 4)) * 2 + kk,
        )

    def wrap(v, n):
        return lax.rem(v + 2 * n, n)

    plane_of = {0: lambda d: at(dx=d), 1: lambda d: at(dy=d)}
    rps, cps = (rp_a, rp_b), (cp_a, cp_b)
    arrivals = [0]
    sent = [0, 0]
    turn = [0]

    def group():
        arrivals[0] += 1
        return arrivals[0] - 1

    def send(src, dst, device, g):
        pltpu.make_async_remote_copy(
            src_ref=src, dst_ref=dst, send_sem=send_sem.at[turn[0]], recv_sem=recv_sem.at[g],
            device_id=device, device_id_type=MESH,
        ).start()
        width = 1 if src.dtype == jnp.bfloat16 else 2
        sent[turn[0]] += width * math.prod(src.shape) // 128

    def take(g, ref):
        pltpu.make_async_remote_copy(
            src_ref=ref, dst_ref=ref, send_sem=send_sem.at[0], recv_sem=recv_sem.at[g],
            device_id=at(flip=True), device_id_type=MESH,
        ).wait_recv()

    def drain(p):
        ref = gone.at[pl.ds(0, sent[p])]
        pltpu.make_async_remote_copy(
            src_ref=ref, dst_ref=ref, send_sem=send_sem.at[p], recv_sem=recv_sem.at[0],
            device_id=at(flip=True), device_id_type=MESH,
        ).wait_send()

    tile_copies = [
        pltpu.make_async_copy(tiles_ref.at[0, 0, s], blocks.at[s], tile_sem.at[0])
        for s in range(SLOTS)
    ]
    diag_copy = pltpu.make_async_copy(diag_ref.at[0], diag, diag_sem.at[0])

    peers = [at(dx=d) for d in STEPS] + [at(dy=d) for d in STEPS]
    peers += [at(dz=d) for d in range(1, 8)] + [at(flip=True)]
    barrier = pltpu.get_barrier_semaphore()
    for peer in peers:
        pl.semaphore_signal(barrier, inc=1, device_id=peer, device_id_type=MESH)
    pl.semaphore_wait(barrier, len(peers))

    def half(h):
        return pl.ds(h * HALF, HALF)

    def gather_begin(p, value):
        rps[p][k, y, x] = value
        cps[p][z] = value
        first = [[group() for _ in STEPS] for _ in range(2)]
        second = [[group() for _ in STEPS] for _ in range(2)]
        far, rest, across = [group(), group()], group(), group()
        own = cps[p].at[z]
        for d, g in ((2, far[0]), (-2, far[1])):
            send(own, own, at(dz=d), g)
        for i, d in enumerate(STEPS):
            for h in range(2):
                own = rps[p].at[k, y, x, half(h)]
                send(own, own, plane_of[h](d), first[h][i])
        own = cps[p].at[z]
        for d in (1, -1):
            send(own, own, at(dz=d), rest)
        for j, e in enumerate(STEPS):
            for h in range(2):
                own = rps[p].at[k, y, x, half(h)]
                send(own, own, plane_of[1 - h](e), second[h][j])
        return first, second, far, rest, across

    def gather_forward(p, state):
        first, second, far, rest, across = state
        for i, d in enumerate(STEPS):
            for h in range(2):
                ty, tx = (y, wrap(x - d, 4)) if h == 0 else (wrap(y - d, 4), x)
                got = rps[p].at[k, ty, tx, half(h)]
                take(first[h][i], got)
                for j, e in enumerate(STEPS):
                    send(got, got, plane_of[1 - h](e), second[h][j])
        for i, d in enumerate((2, -2)):
            got = cps[p].at[wrap(z - d, 8)]
            take(far[i], got)
            send(got, got, at(dz=d // 2), rest)
            got = cps[p].at[wrap(z - d, 8), half(i)]
            send(got, got, at(dz=d), rest)
        for h in range(2):
            line = rps[p].at[k, y, :, half(h)] if h == 0 else rps[p].at[k, :, x, half(h)]
            send(line, line, at(flip=True), across)

    def gather_across(p, state):
        first, second, far, rest, across = state
        for j, e in enumerate(STEPS):
            for h in range(2):
                line = (
                    rps[p].at[k, wrap(y - e, 4), :, half(h)]
                    if h == 0
                    else rps[p].at[k, :, wrap(x - e, 4), half(h)]
                )
                take(second[h][j], line)
                send(line, line, at(flip=True), across)

    def gather_end_z(p, state):
        take(state[3], cps[p].at[pl.ds(0, 5)])

    def gather_end_plane(p, state):
        take(state[4], rps[p].at[1 - k])

    def forward_products(p):
        def step(s, carry):
            far = unpack(cps[p][cols_ref[0, 0, s]])
            seg_r[s] = pack(dot(far, blocks[s], 1, 1)) + seg_r[prev_r[s]]
            return carry

        lax.fori_loop(0, SLOTS, step, 0, unroll=UNROLL)

    def mirror_products(p, low, high, cross):
        count = counts_ref[0, 0]

        def step(s, cross):
            t = rows_ref[0, 0, s]
            near = unpack(rps[p][lax.rem(t, 2), t // 8, lax.rem(t // 2, 4)])
            product = dot(near, blocks[s], 1, 0)
            seg_c[s] = pack(product) + seg_c[prev_c[s]]
            if p == 0:
                kept[s] = product.astype(jnp.bfloat16)
                return cross
            far = unpack(cps[p][cols_ref[0, 0, s]])
            held = jnp.where(s < count, 1.0, 0.0)
            return cross + held * dot(far, product.astype(jnp.bfloat16), 1, 1)

        return lax.fori_loop(low, high, step, cross, unroll=UNROLL)

    def late_cross(p, cross):
        count = counts_ref[0, 0]

        def step(s, cross):
            far = unpack(cps[p][cols_ref[0, 0, s]])
            held = jnp.where(s < count, 1.0, 0.0)
            return cross + held * dot(far, kept[s], 1, 1)

        return lax.fori_loop(0, SLOTS, step, cross, unroll=UNROLL)

    def plane_begin(p):
        def fill(kk):
            @pl.loop(0, 16, unroll=4)
            def _(t):
                ps[p, kk, t // 4, lax.rem(t, 4)] = seg_r[last_r[2 * t + kk]].astype(jnp.bfloat16)

        fill(1 - k)
        across = {}
        for d in ORDER:
            for h in range(2):
                across[h, d] = group()
                if h == 0:
                    t = wrap(x + d, 4)
                    src, dst = ps.at[p, 1 - k, :, t, half(h)], xb.at[p, :, t, half(h)]
                else:
                    t = wrap(y + d, 4)
                    src, dst = ps.at[p, 1 - k, t, :, half(h)], xb.at[p, t, :, half(h)]
                send(src, dst, at(flip=True), across[h, d])
        fill(k)
        return across

    def plane_stage(p, across, d):
        out = []
        for h in range(2):
            if h == 0:
                t, mine = wrap(x + d, 4), y
                take(across[h, d], xb.at[p, :, t, half(h)])
                total = ps[p, k, :, t, half(h)].astype(jnp.float32) + xb[p, :, t, half(h)].astype(jnp.float32)
            else:
                t, mine = wrap(y + d, 4), x
                take(across[h, d], xb.at[p, t, :, half(h)])
                total = ps[p, k, t, :, half(h)].astype(jnp.float32) + xb[p, t, :, half(h)].astype(jnp.float32)
            qb[p, h, d] = total.astype(jnp.bfloat16)
            g = group()
            for e in (2, 1, 3):
                send(qb.at[p, h, d, wrap(mine + e, 4)], r1.at[p, h, d, e - 1], plane_of[1 - h](e), g)
            out.append(g)
        return out

    def plane_stage2(p, mid, hooks):
        last = group()
        own = []
        for d in ORDER:
            for h in range(2):
                take(mid[d][h], r1.at[p, h, d])
                total = qb[p, h, d, y if h == 0 else x].astype(jnp.float32)
                for e in range(3):
                    total = total + r1[p, h, d, e].astype(jnp.float32)
                if d != 0:
                    sb[p, h, d] = total.astype(jnp.bfloat16)
                    send(sb.at[p, h, d], r2.at[p, h, d - 1], plane_of[h](d), last)
                else:
                    own.append(total)
            if d in hooks:
                hooks[d]()
        return last, own

    def plane_end(p, state):
        last, own = state
        take(last, r2.at[p])
        halves = []
        for h in range(2):
            total = own[h]
            for d in range(3):
                total = total + r2[p, h, d].astype(jnp.float32)
            halves.append(total)
        return jnp.concatenate(halves, axis=0)

    def z_begin(p):
        @pl.loop(0, ROWS, unroll=4)
        def _(t):
            pz[p, t] = seg_c[last_c[t]].astype(jnp.bfloat16)

        near, far = [group(), group()], group()
        for i, d in enumerate((1, -1)):
            send(pz.at[p, wrap(z + 3 * d, 8)], zin.at[p, i, pl.ds(0, PK)], at(dz=d), near[i])
            send(pz.at[p, wrap(z + 4, 8), half(i)], zin.at[p, i, pl.ds(PK, HALF)], at(dz=2 * d), near[i])
        for i, d in enumerate((1, -1)):
            send(pz.at[p, wrap(z + d, 8)], zr2.at[p, i], at(dz=d), far)
        return near, far

    def z_stage(p, state):
        near, far = state
        for i, d in enumerate((2, -2)):
            take(near[i], zin.at[p, i])
            total = pz[p, wrap(z + d, 8)].astype(jnp.float32) + zin[p, i, 0:PK].astype(jnp.float32)
            extra = zin[p, i, PK : PK + HALF].astype(jnp.float32)
            lo, hi = total[0:HALF], total[HALF:PK]
            if i == 0:
                lo = lo + extra
            else:
                hi = hi + extra
            zq[p, i, 0:HALF] = lo.astype(jnp.bfloat16)
            zq[p, i, HALF:PK] = hi.astype(jnp.bfloat16)
            send(zq.at[p, i], zr2.at[p, 2 + i], at(dz=d), far)

    def z_end(p, state):
        take(state[1], zr2.at[p])
        total = pz[p, z].astype(jnp.float32)
        for i in range(4):
            total = total + zr2[p, i].astype(jnp.float32)
        return total

    groups = (
        [at(flip=True)],
        [at(dx=d) for d in STEPS],
        [at(dy=d) for d in STEPS],
        [at(dz=d) for d in range(1, 8)],
    )
    bases = (0, 1, 4, 7)

    def reduce_steps(buf, rbuf, value):
        buf[0] = value
        for stage in range(4):
            g = group()
            for i, peer in enumerate(groups[stage]):
                send(buf.at[stage], rbuf.at[bases[stage] + i], peer, g)
            yield None
            total = buf[stage]
            n = len(groups[stage])
            take(g, rbuf.at[pl.ds(bases[stage], n)])
            for i in range(n):
                total = total + rbuf[bases[stage] + i]
            if stage < 3:
                buf[stage + 1] = total
        yield total

    def own_product(v):
        hi = v.astype(jnp.bfloat16)
        lo = (v - hi.astype(jnp.float32)).astype(jnp.bfloat16)
        d = diag[...]
        return dot(hi, d, 1, 1) + dot(lo, d, 1, 1)

    probes = probes_ref[0]
    state = gather_begin(0, pack(probes).astype(jnp.bfloat16))
    diag_copy.start()
    for copy in tile_copies[:8]:
        copy.start()

    count = counts_ref[0, 0]
    for s in range(SLOTS):
        pr = jnp.int32(SLOTS)
        pc = jnp.int32(SLOTS)
        for u in range(s):
            pr = jnp.where(rows_ref[0, 0, u] == rows_ref[0, 0, s], u, pr)
            pc = jnp.where(cols_ref[0, 0, u] == cols_ref[0, 0, s], u, pc)
        prev_r[s] = pr
        prev_c[s] = pc

    @pl.loop(0, PLANE)
    def _(t):
        at_slot = jnp.int32(SLOTS)
        for s in range(SLOTS):
            at_slot = jnp.where((rows_ref[0, 0, s] == t) & (s < count), s, at_slot)
        last_r[t] = at_slot

    @pl.loop(0, ROWS)
    def _(t):
        at_slot = jnp.int32(SLOTS)
        for s in range(SLOTS):
            at_slot = jnp.where((cols_ref[0, 0, s] == t) & (s < count), s, at_slot)
        last_c[t] = at_slot

    seg_r[SLOTS] = jnp.zeros((PK, 128), jnp.float32)
    seg_c[SLOTS] = jnp.zeros((PK, 128), jnp.float32)

    g00 = gram(probes, probes)
    diag_copy.wait()
    trace = jnp.zeros((1, 1), jnp.float32)
    for j in range(5):
        n = 128 if j < 4 else 64
        d = diag[pl.ds(128 * j, n), pl.ds(128 * j, n)].astype(jnp.float32)
        on = lax.broadcasted_iota(jnp.int32, (n, n), 0) == lax.broadcasted_iota(jnp.int32, (n, n), 1)
        trace = trace + jnp.sum(jnp.where(on, d, 0.0), keepdims=True)
    red_a = reduce_steps(
        ar_a, ar_ar, jnp.concatenate([fold(g00), jnp.broadcast_to(trace, (8, 128))], axis=0)
    )
    next(red_a)
    gather_forward(0, state)
    for copy in tile_copies[8:]:
        copy.start()
    next(red_a)
    own = own_product(probes)
    gather_across(0, state)
    next(red_a)
    gather_end_z(0, state)
    pltpu.make_async_copy(tiles_ref.at[0, 0], blocks, tile_sem.at[0]).wait()
    forward_products(0)
    across = plane_begin(0)
    next(red_a)
    gather_end_plane(0, state)
    mid = {}
    cross = mirror_products(0, 0, 12, jnp.zeros((Q, Q), jnp.float32))
    mid[2] = plane_stage(0, across, 2)
    cross = mirror_products(0, 12, 16, cross)
    zs = z_begin(0)
    mid[1] = plane_stage(0, across, 1)
    mid[3] = plane_stage(0, across, 3)
    mid[0] = plane_stage(0, across, 0)
    cross = late_cross(0, cross)
    cross = cross + cross.T
    red_b = reduce_steps(ar_b, ar_br, fold(gram(probes, own) + cross))
    next(red_b)
    total = next(red_a)
    rr0 = unfold(total[0:32])
    shift = total[32:33, 0:1] * (1.0 / (NT * B))
    eye = (
        lax.broadcasted_iota(jnp.int32, (Q, Q), 0) == lax.broadcasted_iota(jnp.int32, (Q, Q), 1)
    ).astype(jnp.float32)
    offset = pack(own - shift * probes)
    next(red_b)
    z_stage(0, zs)
    last = plane_stage2(0, mid, {1: lambda: next(red_b), 3: lambda: next(red_b)})
    packed = offset + z_end(0, zs)
    packed = packed + plane_end(0, last)

    turn[0] = 1
    state = gather_begin(1, packed.astype(jnp.bfloat16))
    basis = unpack(packed)
    image = basis + shift * probes
    red_c = reduce_steps(ar_c, ar_cr, fold(gram(basis, basis)))
    next(red_c)
    rr0_inv = solve(rr0, eye)
    gather_forward(1, state)
    next(red_c)
    own = own_product(basis)
    pq0 = unfold(next(red_b))
    alpha = solve(pq0, rr0)
    drain(0)
    gather_across(1, state)
    next(red_c)
    gather_end_z(1, state)
    forward_products(1)
    across = plane_begin(1)
    next(red_c)
    gather_end_plane(1, state)
    mid = {}
    cross = mirror_products(1, 0, 12, jnp.zeros((Q, Q), jnp.float32))
    mid[2] = plane_stage(1, across, 2)
    cross = mirror_products(1, 12, 16, cross)
    cross = cross + cross.T
    zs = z_begin(1)
    red_d = reduce_steps(ar_d, ar_dr, fold(gram(basis, own) + cross))
    next(red_d)
    mid[1] = plane_stage(1, across, 1)
    mid[3] = plane_stage(1, across, 3)
    mid[0] = plane_stage(1, across, 0)
    next(red_d)
    g11 = unfold(next(red_c))
    g01 = pq0 - shift * rr0
    m0 = eye - shift * alpha
    m1 = -alpha
    rr1 = (
        dot_hi(m0, dot_hi(rr0, m0, 1, 0) + dot_hi(g01, m1, 1, 0), 0, 0)
        + dot_hi(m1, dot_hi(g01, m0, 0, 0) + dot_hi(g11, m1, 1, 0), 0, 0)
    )
    beta = dot_hi(rr0_inv, rr1, 1, 0)
    n0 = m0 + beta
    next(red_d)
    g02 = g11 + shift * g01
    known = dot_hi(n0, dot_hi(pq0, n0, 1, 0) + dot_hi(g02, m1, 1, 0), 0, 0) + dot_hi(
        m1, dot_hi(g02, n0, 0, 0), 0, 0
    )
    z_stage(1, zs)
    next(red_d)
    found = []

    def finish():
        residual = combine(m0, probes) + combine(m1, basis)
        direction = residual + combine(beta, probes)
        xsol = combine(alpha, probes)
        partial = combine(n0, image) + combine(m1, own)
        g12 = unfold(next(red_d))
        gamma = solve(known + dot_hi(m1, dot_hi(g12, m1, 1, 0), 0, 0), rr1)
        found.extend((residual, direction, xsol, partial, gamma))

    last = plane_stage2(1, mid, {3: finish})
    drain(1)
    residual, direction, xsol, partial, gamma = found
    deep = z_end(1, zs)
    deep = deep + plane_end(1, last)
    image2 = partial + combine(m1, unpack(deep))
    sol_ref[...] = xsol + combine(gamma, direction)
    res_ref[...] = residual - combine(gamma, image2)


def close(sol_ref, res_ref, sol_out, res_out):
    sol_out[0] = sol_ref[...]
    res_out[0] = res_ref[...]


def body(tiles, diag_tiles, probes, rows_list, cols_list, counts):
    smem = pl.BlockSpec(memory_space=pltpu.SMEM)
    vmem = pl.BlockSpec(memory_space=pltpu.VMEM)
    hbm = pl.BlockSpec(memory_space=pl.ANY)
    bf, f32, i32 = jnp.bfloat16, jnp.float32, jnp.int32
    wide = jax.ShapeDtypeStruct((Q, B), f32)
    parts = pl.pallas_call(
        kernel,
        out_shape=(wide, wide),
        in_specs=[smem, smem, smem, hbm, hbm, vmem],
        out_specs=(vmem, vmem),
        scratch_shapes=[
            pltpu.VMEM((SLOTS, B, B), bf),
            pltpu.VMEM((B, B), bf),
            pltpu.VMEM((2, 4, 4, PK, 128), bf),
            pltpu.VMEM((2, 4, 4, PK, 128), bf),
            pltpu.VMEM((ROWS, PK, 128), bf),
            pltpu.VMEM((ROWS, PK, 128), bf),
            pltpu.VMEM((2, 2, 4, 4, PK, 128), bf),
            pltpu.VMEM((2, 4, 4, PK, 128), bf),
            pltpu.VMEM((2, 2, 4, 4, HALF, 128), bf),
            pltpu.VMEM((2, 2, 4, 3, HALF, 128), bf),
            pltpu.VMEM((2, 2, 4, HALF, 128), bf),
            pltpu.VMEM((2, 2, 3, HALF, 128), bf),
            pltpu.VMEM((2, ROWS, PK, 128), bf),
            pltpu.VMEM((2, 2, PK, 128), bf),
            pltpu.VMEM((2, 2, PK + HALF, 128), bf),
            pltpu.VMEM((2, 4, PK, 128), bf),
            pltpu.VMEM((SENT, 128), bf),
            pltpu.VMEM((SLOTS, Q, B), bf),
            pltpu.VMEM((SLOTS + 1, PK, 128), f32),
            pltpu.VMEM((SLOTS + 1, PK, 128), f32),
            pltpu.SMEM((SLOTS,), i32),
            pltpu.SMEM((SLOTS,), i32),
            pltpu.SMEM((PLANE,), i32),
            pltpu.SMEM((ROWS,), i32),
            pltpu.VMEM((4, 40, 128), f32),
            pltpu.VMEM((14, 40, 128), f32),
            pltpu.VMEM((4, 32, 128), f32),
            pltpu.VMEM((14, 32, 128), f32),
            pltpu.VMEM((4, 32, 128), f32),
            pltpu.VMEM((14, 32, 128), f32),
            pltpu.VMEM((4, 32, 128), f32),
            pltpu.VMEM((14, 32, 128), f32),
            pltpu.SemaphoreType.DMA((2,)),
            pltpu.SemaphoreType.DMA((N_ARRIVALS,)),
            pltpu.SemaphoreType.DMA((1,)),
            pltpu.SemaphoreType.DMA((1,)),
        ],
        compiler_params=pltpu.CompilerParams(
            collective_id=0, has_side_effects=True, vmem_limit_bytes=56 << 20
        ),
        name="block_cg",
    )(rows_list, cols_list, counts, tiles, diag_tiles, probes)
    return pl.pallas_call(
        close,
        out_shape=(jax.ShapeDtypeStruct((1, Q, B), f32),) * 2,
        in_specs=[vmem] * 2,
        out_specs=(vmem, vmem),
        name="close",
    )(*parts)


def solution(mesh):
    placed = (
        P("row", "col", None, None, None),
        P(("row", "col"), None, None),
        P(("row", "col"), None, None),
        P("row", "col", None),
        P("row", "col", None),
        P("row", "col"),
    )
    return jax.shard_map(
        body,
        mesh=mesh,
        in_specs=placed,
        out_specs=(P(("row", "col"), None, None), P(("row", "col"), None, None)),
        check_vma=False,
    )
```
